32 devices in a mesh: expert: 8 (over y, x, core), tensor: 4 (over z).
Axes of the slice: x: 2, y: 2, z: 4, core: 2. Of those that a mesh axis runs over, the one named last changes fastest.
Arguments:
- tokens: bfloat16 [8192, 1024], P('expert'), may hold values from -6 to 6
- cotangent: bfloat16 [8192, 1024], P('expert'), may hold values from -6 to 6
- routes: int32 [8192], P('expert'), may hold values from 0 to 15, as said below
- slot_index: int32 [8192], P('expert'), may hold values from 0 to 128, as said below
- first_gain: float32 [1024], replicated, may hold values from 0.1 to 1.9
- first_shift: float32 [1024], replicated, may hold values from -1.25 to 1.25
- project_in: bfloat16 [1024, 3, 1024], P(None, None, 'tensor'), may hold values from -0.25 to 0.25
- project_out: bfloat16 [1024, 1024], P('tensor'), may hold values from -1.5 to 1.5
- second_gain: float32 [1024], replicated, may hold values from 0.1 to 1.9
- second_shift: float32 [1024], replicated, may hold values from -1.25 to 1.25
- router_weight: bfloat16 [1024, 16], replicated, may hold values from -0.09375 to 0.09375
- mixing_weight: bfloat16 [1024, 2], replicated, may hold values from -0.1875 to 0.1875
- dense_up: bfloat16 [1024, 4096], P(None, 'tensor'), may hold values from -0.1875 to 0.1875
- dense_down: bfloat16 [4096, 1024], P('tensor'), may hold values from -0.1875 to 0.1875
- expert_up: bfloat16 [16, 1024, 4096], P('expert', None, 'tensor'), may hold values from -0.375 to 0.375
- expert_down: bfloat16 [16, 4096, 1024], P('expert', 'tensor'), may hold values from -3 to 3
Outputs:
- layer_out: bfloat16 [8192, 1024], P('expert')
- input_grad: bfloat16 [8192, 1024], P('expert')
- first_gain_grad: float32 [1024], replicated
- first_shift_grad: float32 [1024], replicated
- project_in_grad: float32 [1024, 3, 1024], P(None, None, 'tensor')
- project_out_grad: float32 [1024, 1024], P('tensor')
- second_gain_grad: float32 [1024], replicated
- second_shift_grad: float32 [1024], replicated
- router_grad: float32 [1024, 16], replicated
- mixing_grad: float32 [1024, 2], replicated
- dense_up_grad: float32 [1024, 4096], P(None, 'tensor')
- dense_down_grad: float32 [4096, 1024], P('tensor')
- expert_up_grad: float32 [16, 1024, 4096], P('expert', None, 'tensor')
- expert_down_grad: float32 [16, 4096, 1024], P('expert', 'tensor')
The draws below stay inside these ranges and needn't reach their ends.
Inputs may be any that keep to these rules, and one draw needn't show every extreme that they name: `routes`: in every block of 1024 tokens (tokens b * 1024 to (b + 1) * 1024 - 1) some expert is named by more than 128 tokens. slot_index[t] is the number of earlier tokens of t's block with the same route, or 128 where that number is 128 or more (the token is dropped); so at most 128 kept tokens of a block name one expert, and every block fills all 128 slots of some expert.
All inputs are finite; a program needn't handle non-finite values.
Results may differ from the reference program's by a relative error of at most 0.023.
Values may be sent and summed in bfloat16 or wider, within the bound.
No kernel may reach another device: no remote copies, remote signals or barrier semaphores. Data moves between devices by JAX's collectives and lax.ppermute only.
A program may use at most 192 MiB of HBM per device.

```python
from functools import partial
import jax
import jax.numpy as jnp
from jax import lax

D = 1024
HEADS = 16
HEAD_DIM = 64
FF = 4096
SEQ = 1024
TOK_DEV = 1024
TOKENS = 8192
EXPERTS = 16
CAP = 128
N_EXPERT = 8


def block_routes(block_key):
    key_base, key_rank, key_order, key_count = jax.random.split(block_key, 4)
    picked = jax.random.randint(key_base, (TOK_DEV,), 0, EXPERTS, dtype=jnp.int32)
    ranking = jax.random.permutation(key_rank, EXPERTS).astype(jnp.int32)
    full_count = jax.random.randint(key_count, (), 1, EXPERTS // 4 + 1, dtype=jnp.int32)
    order = jax.random.permutation(key_order, TOK_DEV).astype(jnp.int32)
    position = jnp.zeros((TOK_DEV,), jnp.int32).at[order].set(jnp.arange(TOK_DEV, dtype=jnp.int32))
    group = jnp.where(position < 2 * CAP, 0, 1 + (position - 2 * CAP) // CAP).astype(jnp.int32)
    used = group < full_count
    target = jnp.take(ranking, jnp.minimum(group, EXPERTS - 1), axis=0)
    chosen = jnp.where(used, target, picked).astype(jnp.int32)
    onehot = (chosen[:, None] == jnp.arange(EXPERTS, dtype=jnp.int32)[None, :]).astype(jnp.int32)
    before = jnp.cumsum(onehot, axis=0) - onehot
    ranked = jnp.sum(before * onehot, axis=1).astype(jnp.int32)
    return (chosen, jnp.minimum(ranked, CAP).astype(jnp.int32))


def routing_plan(key):
    blocks = TOKENS // TOK_DEV
    base_key = jax.random.fold_in(key, 17)
    block_keys = jax.random.split(base_key, blocks)
    chosen, ranked = jax.vmap(block_routes)(block_keys)
    return (chosen.reshape(TOKENS).astype(jnp.int32), ranked.reshape(TOKENS).astype(jnp.int32))


def draw_routes(key, part):
    return routing_plan(key)[0]


def draw_slot_index(key, part):
    return routing_plan(key)[1]


def steps_of(key, extent, pieces, low, top_value):
    loudness, own = 1.0, jax.random.fold_in(key, 6)
    for dim, shards_of in pieces:
        draws = jnp.exp(jax.random.uniform(jax.random.fold_in(own, dim), (shards_of,), jnp.float32, low / len(pieces), top_value / len(pieces)))
        loudness = loudness * jnp.repeat(draws, extent[dim] // shards_of).reshape([-1 if axis == dim else 1 for axis in range(len(extent))])
    return loudness


def bell_draw(stream_key, shape, scale, reach, cuts=(), kind=jnp.bfloat16):
    entries = scale * jax.random.normal(stream_key, shape, jnp.float32)
    if cuts:
        entries = entries * steps_of(stream_key, shape, cuts, -0.22, 0.18)
    return jnp.clip(entries, -reach, reach).astype(kind)


def setup_inputs(seed: int = 0) -> dict:
    keys = jax.random.split(jax.random.key(seed), 17)
    tokens = bell_draw(keys[0], (TOKENS, D), 1.0, 6.0, ((0, 8),))
    cotangent = bell_draw(keys[1], (TOKENS, D), 1.0, 6.0, ((0, 8),))
    routes = draw_routes(jax.random.fold_in(keys[16], 71), 0)
    slot_index = draw_slot_index(jax.random.fold_in(keys[16], 71), 0)
    first_gain = jnp.clip(1.0 + 0.18 * jax.random.normal(keys[4], (D,), jnp.float32), 0.1, 1.9)
    first_shift = bell_draw(keys[5], (D,), 0.2, 1.25, (), jnp.float32)
    project_in = bell_draw(keys[6], (D, 3, D), (D // 2) ** -0.5, 0.25, ((2, 4),))
    project_out = bell_draw(keys[7], (D, D), (D // 64) ** -0.5, 1.5, ((0, 4),))
    second_gain = jnp.clip(1.0 + 0.18 * jax.random.normal(keys[8], (D,), jnp.float32), 0.1, 1.9)
    second_shift = bell_draw(keys[9], (D,), 0.2, 1.25, (), jnp.float32)
    router_weight = bell_draw(keys[10], (D, EXPERTS), (4 * D) ** -0.5, 0.09375)
    mixing_weight = bell_draw(keys[11], (D, 2), D ** -0.5, 0.1875)
    dense_up = bell_draw(keys[12], (D, FF), D ** -0.5, 0.1875, ((1, 4),))
    dense_down = bell_draw(keys[13], (FF, D), (FF // 4) ** -0.5, 0.1875, ((0, 4),))
    expert_up = bell_draw(keys[14], (EXPERTS, D, FF), (D // 4) ** -0.5, 0.375, ((0, 8), (2, 4)))
    expert_down = bell_draw(keys[15], (EXPERTS, FF, D), (max(1, FF // (4 * EXPERTS * EXPERTS))) ** -0.5, 3.0, ((0, 8), (1, 4)))
    return {"tokens": tokens, "cotangent": cotangent, "routes": routes, "slot_index": slot_index, "first_gain": first_gain, "first_shift": first_shift, "project_in": project_in, "project_out": project_out, "second_gain": second_gain, "second_shift": second_shift, "router_weight": router_weight, "mixing_weight": mixing_weight, "dense_up": dense_up, "dense_down": dense_down, "expert_up": expert_up, "expert_down": expert_down}


@jax.custom_vjp
def low(v):
    return lax.optimization_barrier(v.astype(jnp.bfloat16)).astype(jnp.float32)

@jax.custom_vjp
def low_back(v):
    return v

def low_keep(v):
    return (low(v), None)

def low_pass(kept, grad):
    return (grad,)

def back_keep(v):
    return (v, None)

def back_low(kept, grad):
    return (low(grad),)
low.defvjp(low_keep, low_pass)
low_back.defvjp(back_keep, back_low)
EPS = 1e-05
HIGH = lax.Precision.HIGHEST

def layer_norm(row_values, norm_gain, norm_shift):
    row_mean = lax.optimization_barrier(jnp.mean(row_values, axis=-1, keepdims=True))
    centred = row_values - row_mean
    spread = lax.optimization_barrier(jnp.mean(centred * centred, axis=-1, keepdims=True))
    return centred * lax.rsqrt(spread + EPS) * norm_gain + norm_shift

def gelu_tanh(values):
    return jax.nn.gelu(values, approximate=True)

def attend(packed):
    queries = packed[:, 0]
    key_rows = packed[:, 1]
    values = packed[:, 2]
    scores = jnp.einsum('qhd,khd->hqk', queries, key_rows, precision=HIGH) * HEAD_DIM ** (-0.5)
    scores = low_back(scores)
    places = jnp.arange(SEQ, dtype=jnp.int32)
    allowed = places[None, :] <= places[:, None]
    scores = jnp.where(allowed[None], scores, -1e+30)
    weights = low(jax.nn.softmax(scores, axis=-1))
    return jnp.einsum('hqk,khd->qhd', weights, values, precision=HIGH)

def expert_rows(packed):
    row_values, up_weight, down_weight = packed
    pre_act = low_back(jnp.dot(row_values, up_weight, precision=HIGH))
    hidden = low(gelu_tanh(pre_act))
    return jnp.dot(hidden, down_weight, precision=HIGH)

def forward(routes, slot_index, inputs, first_gain, first_shift, project_in, project_out, second_gain, second_shift, router_weight, mixing_weight, dense_up, dense_down, expert_up, expert_down):
    normed_in = low(layer_norm(inputs, first_gain, first_shift))
    projected = jnp.einsum('td,dcn->tcn', normed_in, project_in, precision=HIGH)
    projected = low_back(low(projected))
    grouped = projected.reshape(TOKENS // SEQ, SEQ, 3, HEADS, HEAD_DIM)
    attended = lax.map(jax.checkpoint(attend), grouped)
    attended = low_back(low(attended.reshape(TOKENS, D)))
    attn_out = low_back(jnp.dot(attended, project_out, precision=HIGH))
    residual = inputs + attn_out
    normed_mid = low(layer_norm(residual, second_gain, second_shift))
    router_logits = low_back(jnp.dot(normed_mid, router_weight, precision=HIGH))
    mixing_logits = low_back(jnp.dot(normed_mid, mixing_weight, precision=HIGH))
    router_probs = jax.nn.softmax(router_logits, axis=-1)
    gate_value = jnp.take_along_axis(router_probs, routes[:, None], axis=1)[:, 0]
    mixing = jax.nn.softmax(mixing_logits, axis=-1)
    dense_pre = low_back(jnp.dot(normed_mid, dense_up, precision=HIGH))
    dense_hidden = low(gelu_tanh(dense_pre))
    dense_out = low_back(jnp.dot(dense_hidden, dense_down, precision=HIGH))
    slot_total = EXPERTS * N_EXPERT * CAP
    block_of = jnp.arange(TOKENS, dtype=jnp.int32) // TOK_DEV
    kept = slot_index < CAP
    slot_place = jnp.where(kept, routes * (N_EXPERT * CAP) + block_of * CAP + slot_index, slot_total).astype(jnp.int32)
    holder = jnp.full((slot_total,), TOKENS, dtype=jnp.int32).at[slot_place].set(jnp.arange(TOKENS, dtype=jnp.int32), mode='drop')
    padded = jnp.concatenate([normed_mid, jnp.zeros((1, D), normed_mid.dtype)], axis=0)
    expert_in = padded[holder].reshape(EXPERTS, N_EXPERT * CAP, D)
    expert_out = lax.map(jax.checkpoint(expert_rows), (expert_in, expert_up, expert_down))
    expert_out = low_back(expert_out)
    flat_out = jnp.concatenate([expert_out.reshape(slot_total, D), jnp.zeros((1, D), expert_out.dtype)], axis=0)
    expert_tok = flat_out[slot_place]
    return residual + mixing[:, 0:1] * dense_out + (mixing[:, 1] * gate_value)[:, None] * expert_tok

def reference(tokens, cotangent, routes, slot_index, first_gain, first_shift, project_in, project_out, second_gain, second_shift, router_weight, mixing_weight, dense_up, dense_down, expert_up, expert_down):
    layer_out, backward = jax.vjp(partial(forward, routes, slot_index), tokens.astype(jnp.float32), first_gain.astype(jnp.float32), first_shift.astype(jnp.float32), project_in.astype(jnp.float32), project_out.astype(jnp.float32), second_gain.astype(jnp.float32), second_shift.astype(jnp.float32), router_weight.astype(jnp.float32), mixing_weight.astype(jnp.float32), dense_up.astype(jnp.float32), dense_down.astype(jnp.float32), expert_up.astype(jnp.float32), expert_down.astype(jnp.float32))
    gradients = backward(cotangent.astype(jnp.float32))
    return (layer_out.astype(jnp.bfloat16), gradients[0].astype(jnp.bfloat16), gradients[1], gradients[2], gradients[3], gradients[4], gradients[5], gradients[6], gradients[7], gradients[8], gradients[9], gradients[10], gradients[11], gradients[12])
```

```python
import functools

import jax
import jax.numpy as jnp
from jax import lax
from jax.experimental import pallas as pl
from jax.experimental.pallas import tpu as pltpu
from jax.sharding import PartitionSpec as P

HEAD_DIM = 64
EPS = 1e-05
NEGATIVE = -1e30
BF = jnp.bfloat16
F32 = jnp.float32


def norm_stats(rows):
    row_mean = jnp.mean(rows, axis=-1, keepdims=True)
    centred = rows - row_mean
    spread = jnp.mean(centred * centred, axis=-1, keepdims=True)
    inverse = lax.rsqrt(spread + EPS)
    return centred * inverse, inverse


def norm_back(unit, inverse, gain, grad):
    weighted = grad * gain
    first = jnp.mean(weighted, axis=-1, keepdims=True)
    second = jnp.mean(weighted * unit, axis=-1, keepdims=True)
    return inverse * (weighted - first - unit * second)


def gelu_both(v):
    inner = 0.7978845608 * (v + 0.044715 * v * v * v)
    bent = jnp.tanh(inner)
    value = 0.5 * v * (1.0 + bent)
    slope = 0.5 * (1.0 + bent) + 0.5 * v * (1.0 - bent * bent) * 0.7978845608 * (
        1.0 + 3.0 * 0.044715 * v * v
    )
    return value, slope


def t_dot(a, b):
    return lax.dot_general(a, b, (((0,), (0,)), ((), ())), preferred_element_type=F32)


def after(value, *others):
    return lax.optimization_barrier((value,) + others)[0]


def dot(a, b):
    return jnp.dot(a, b, preferred_element_type=F32)

def dot_t(a, b):
    return lax.dot_general(a, b, (((1,), (1,)), ((), ())), preferred_element_type=F32)

def head_lanes(head, rows):
    lanes = lax.broadcasted_iota(jnp.int32, (rows, 2 * HEAD_DIM), 1)
    return (lanes < HEAD_DIM) if head == 0 else (lanes >= HEAD_DIM)

def keep_causal(scores, tile):
    keys = scores.shape[0]
    key_pos = lax.broadcasted_iota(jnp.int32, (tile, tile), 0)
    query_pos = lax.broadcasted_iota(jnp.int32, (tile, tile), 1)
    last = jnp.where(key_pos <= query_pos, scores[keys - tile :], NEGATIVE)
    if keys == tile:
        return last
    return jnp.concatenate([scores[: keys - tile], last], axis=0)

def attend_forward_kernel(tile, qkv_ref, out_ref, log_ref):
    rows = qkv_ref.shape[1]
    values_t = jnp.transpose(qkv_ref[2])
    for block in range(rows // tile):
        keys = (block + 1) * tile
        here = pl.ds(block * tile, tile)
        query_block = qkv_ref[0, here, :]
        pieces, logs = [], []
        for head in range(2):
            q = jnp.where(head_lanes(head, tile), query_block, jnp.zeros_like(query_block))
            scores = dot_t(qkv_ref[1, :keys, :], q) * (HEAD_DIM ** (-0.5))
            scores = keep_causal(scores, tile)
            top = jnp.max(scores, axis=0, keepdims=True)
            powers = jnp.exp(scores - top)
            total = jnp.sum(powers, axis=0, keepdims=True)
            blended = dot(values_t[head * HEAD_DIM : (head + 1) * HEAD_DIM, :keys], powers.astype(BF))
            pieces.append(blended / total)
            logs.append(top + jnp.log(total))
        out_ref[here, :] = jnp.transpose(jnp.concatenate(pieces, axis=0)).astype(BF)
        for head in range(2):
            log_ref[0, head : head + 1, here] = logs[head]

def attend_backward_kernel(tile, qkv_ref, log_ref, grad_ref, out_ref, key_acc, value_acc):
    rows = qkv_ref.shape[1]
    scale = HEAD_DIM ** (-0.5)
    keys_t = jnp.transpose(qkv_ref[1])
    count = rows // tile
    for block in reversed(range(count)):
        keys = (block + 1) * tile
        here = pl.ds(block * tile, tile)
        query_block = qkv_ref[0, here, :]
        grad_block = grad_ref[here, :]
        pieces = []
        for head in range(2):
            lanes = head_lanes(head, tile)
            q = jnp.where(lanes, query_block, jnp.zeros_like(query_block))
            g = jnp.where(lanes, grad_block, jnp.zeros_like(grad_block))
            scores = dot_t(qkv_ref[1, :keys, :], q) * scale
            scores = keep_causal(scores, tile)
            weights = jnp.exp(scores - log_ref[0, head : head + 1, here])
            weight_grad = dot_t(qkv_ref[2, :keys, :], g)
            inner = jnp.sum(weights * weight_grad, axis=0, keepdims=True)
            score_grad = (weights * (weight_grad - inner)).astype(BF)
            key_step = dot(score_grad, q)
            value_step = dot(weights.astype(BF), g)
            if block == count - 1 and head == 0:
                key_acc[...] = key_step
                value_acc[...] = value_step
            else:
                key_acc[:keys, :] += key_step
                value_acc[:keys, :] += value_step
            pieces.append(dot(keys_t[head * HEAD_DIM : (head + 1) * HEAD_DIM, :keys], score_grad))
        out_ref[0, here, :] = (jnp.transpose(jnp.concatenate(pieces, axis=0)) * scale).astype(BF)
    out_ref[1] = (key_acc[...] * scale).astype(BF)
    out_ref[2] = value_acc[...].astype(BF)

def attend_forward(qkv, tile=256):
    _, rows, columns = qkv.shape
    pairs = columns // (2 * HEAD_DIM)
    return pl.pallas_call(
        functools.partial(attend_forward_kernel, tile),
        grid=(pairs,),
        out_shape=(
            jax.ShapeDtypeStruct((rows, columns), BF),
            jax.ShapeDtypeStruct((pairs, 8, rows), F32),
        ),
        in_specs=[pl.BlockSpec((3, rows, 2 * HEAD_DIM), lambda p: (0, 0, p))],
        out_specs=(
            pl.BlockSpec((rows, 2 * HEAD_DIM), lambda p: (0, p)),
            pl.BlockSpec((1, 8, rows), lambda p: (p, 0, 0)),
        ),
        cost_estimate=pl.CostEstimate(
            flops=8 * rows * rows * columns // 2, bytes_accessed=8 * rows * columns,
            transcendentals=rows * rows * columns // 128),
        name="attend_forward",
    )(qkv)

def attend_backward(qkv, logs, grads, tile=256):
    _, rows, columns = qkv.shape
    pairs = columns // (2 * HEAD_DIM)
    return pl.pallas_call(
        functools.partial(attend_backward_kernel, tile),
        grid=(pairs,),
        out_shape=jax.ShapeDtypeStruct((3, rows, columns), BF),
        in_specs=[
            pl.BlockSpec((3, rows, 2 * HEAD_DIM), lambda p: (0, 0, p)),
            pl.BlockSpec((1, 8, rows), lambda p: (p, 0, 0)),
            pl.BlockSpec((rows, 2 * HEAD_DIM), lambda p: (0, p)),
        ],
        out_specs=pl.BlockSpec((3, rows, 2 * HEAD_DIM), lambda p: (0, 0, p)),
        scratch_shapes=[pltpu.VMEM((rows, 2 * HEAD_DIM), F32)] * 2,
        cost_estimate=pl.CostEstimate(
            flops=20 * rows * rows * columns // 2, bytes_accessed=16 * rows * columns,
            transcendentals=rows * rows * columns // 128),
        name="attend_backward",
    )(qkv, logs, grads)


def project_kernel(heads_ref, weight_ref, token_ref, gain_ref, shift_ref, rest_ref, low_ref):
    total = token_ref[...].astype(F32)
    for z in range(heads_ref.shape[0]):
        total = total + dot(heads_ref[z], weight_ref[z])
    rest_ref[...] = total
    unit, _ = norm_stats(total)
    low_ref[...] = (unit * gain_ref[...] + shift_ref[...]).astype(BF)


def project_norm(heads, weight, tokens, gain, shift, tile=256):
    parts, rows, columns = heads.shape
    width = weight.shape[2]
    block = lambda i: (i, 0)
    return pl.pallas_call(
        project_kernel,
        grid=(rows // tile,),
        out_shape=(
            jax.ShapeDtypeStruct((rows, width), F32),
            jax.ShapeDtypeStruct((rows, width), BF),
        ),
        in_specs=[
            pl.BlockSpec((parts, tile, columns), lambda i: (0, i, 0)),
            pl.BlockSpec((parts, columns, width), lambda i: (0, 0, 0)),
            pl.BlockSpec((tile, width), block),
            pl.BlockSpec((1, width), lambda i: (0, 0)),
            pl.BlockSpec((1, width), lambda i: (0, 0)),
        ],
        out_specs=(pl.BlockSpec((tile, width), block), pl.BlockSpec((tile, width), block)),
        cost_estimate=pl.CostEstimate(
            flops=2 * rows * parts * columns * width,
            bytes_accessed=12 * rows * width,
            transcendentals=rows,
        ),
        name="project_norm",
    )(heads, weight, tokens, gain[None], shift[None])


def gelu_back_kernel(rows_ref, up_ref, hidden_grad_ref, hidden_ref, pre_grad_ref, in_ref, dot_ref):
    shape = rows_ref.shape
    count = shape[0] * shape[2]
    hidden, slope = gelu_both(dot(rows_ref[...].reshape(count, shape[3]), up_ref[0]))
    hidden = hidden.astype(BF)
    hidden_ref[0] = hidden
    hidden_grad = hidden_grad_ref[0].astype(F32)
    pre_grad = (hidden_grad * slope).astype(BF)
    pre_grad_ref[0] = pre_grad
    in_ref[...] = dot_t(pre_grad, up_ref[0]).astype(BF).reshape(shape)
    dots = jnp.sum(hidden.astype(F32) * hidden_grad, axis=1, keepdims=True)
    dot_ref[0] = jnp.broadcast_to(dots, (count, 128))


def expert_back(arrived, expert_up, hidden_grads, tile=512):
    blocks, held, capacity, width = arrived.shape
    rows = blocks * capacity
    units = expert_up.shape[2]
    slots = pl.BlockSpec((tile // capacity, 1, capacity, width), lambda e, i: (i, e, 0, 0))
    flat = pl.BlockSpec((1, tile, units), lambda e, i: (e, i, 0))
    return pl.pallas_call(
        gelu_back_kernel,
        grid=(held, rows // tile),
        out_shape=(
            jax.ShapeDtypeStruct((held, rows, units), BF),
            jax.ShapeDtypeStruct((held, rows, units), BF),
            jax.ShapeDtypeStruct(arrived.shape, BF),
            jax.ShapeDtypeStruct((held, rows, 128), F32),
        ),
        in_specs=[slots, pl.BlockSpec((1, width, units), lambda e, i: (e, 0, 0)), flat],
        out_specs=(flat, flat, slots, pl.BlockSpec((1, tile, 128), lambda e, i: (e, i, 0))),
        cost_estimate=pl.CostEstimate(
            flops=4 * held * rows * units * width,
            bytes_accessed=14 * held * rows * width,
            transcendentals=held * rows * units,
        ),
        name="expert_back",
    )(arrived, expert_up, hidden_grads)


def down_kernel(hidden_ref, down_ref, out_ref):
    out_ref[...] = dot(hidden_ref[0], down_ref[0]).astype(BF).reshape(out_ref.shape)


def expert_down_rows(hidden, expert_down, blocks, tile=512):
    held, rows, units = hidden.shape
    capacity = rows // blocks
    width = expert_down.shape[2]
    return pl.pallas_call(
        down_kernel,
        grid=(held, rows // tile),
        out_shape=jax.ShapeDtypeStruct((blocks, held, capacity, width), BF),
        in_specs=[
            pl.BlockSpec((1, tile, units), lambda e, i: (e, i, 0)),
            pl.BlockSpec((1, units, width), lambda e, i: (e, 0, 0)),
        ],
        out_specs=pl.BlockSpec(
            (tile // capacity, 1, capacity, width), lambda e, i: (i, e, 0, 0)
        ),
        cost_estimate=pl.CostEstimate(
            flops=2 * held * rows * units * width,
            bytes_accessed=6 * held * rows * width,
            transcendentals=0,
        ),
        name="expert_down_rows",
    )(hidden, expert_down)


def hidden_grad_kernel(grads_ref, down_ref, out_ref):
    shape = grads_ref.shape
    rows = grads_ref[...].reshape(shape[0] * shape[2], shape[3])
    out_ref[0] = dot_t(rows, down_ref[0]).astype(BF)


def expert_hidden_grad(cotan_slots, expert_down, tile=512):
    blocks, held, capacity, width = cotan_slots.shape
    rows = blocks * capacity
    units = expert_down.shape[1]
    return pl.pallas_call(
        hidden_grad_kernel,
        grid=(held, rows // tile),
        out_shape=jax.ShapeDtypeStruct((held, rows, units), BF),
        in_specs=[
            pl.BlockSpec((tile // capacity, 1, capacity, width), lambda e, i: (i, e, 0, 0)),
            pl.BlockSpec((1, units, width), lambda e, i: (e, 0, 0)),
        ],
        out_specs=pl.BlockSpec((1, tile, units), lambda e, i: (e, i, 0)),
        cost_estimate=pl.CostEstimate(
            flops=2 * held * rows * units * width,
            bytes_accessed=6 * held * rows * width,
            transcendentals=0,
        ),
        name="expert_hidden_grad",
    )(cotan_slots, expert_down)


def normed_kernel(grad_ref, weight_ref, token_ref, out_ref, sums_ref):
    total = dot_t(grad_ref[0], weight_ref[0])
    for c in range(1, grad_ref.shape[0]):
        total = total + dot_t(grad_ref[c], weight_ref[c])
    out_ref[...] = total.astype(BF)
    unit, _ = norm_stats(token_ref[...].astype(F32))

    @pl.when(pl.program_id(0) == 0)
    def _():
        sums_ref[...] = jnp.zeros_like(sums_ref)

    sums_ref[0:1, :] += jnp.sum(total * unit, axis=0, keepdims=True)
    sums_ref[1:2, :] += jnp.sum(total, axis=0, keepdims=True)


def normed_back(qkv_grad, project_in, tokens, tile=256):
    count, rows, columns = qkv_grad.shape
    width = project_in.shape[1]
    return pl.pallas_call(
        normed_kernel,
        grid=(rows // tile,),
        out_shape=(
            jax.ShapeDtypeStruct((rows, width), BF),
            jax.ShapeDtypeStruct((8, width), F32),
        ),
        in_specs=[
            pl.BlockSpec((count, tile, columns), lambda i: (0, i, 0)),
            pl.BlockSpec((count, width, columns), lambda i: (0, 0, 0)),
            pl.BlockSpec((tile, width), lambda i: (i, 0)),
        ],
        out_specs=(
            pl.BlockSpec((tile, width), lambda i: (i, 0)),
            pl.BlockSpec((8, width), lambda i: (0, 0)),
        ),
        cost_estimate=pl.CostEstimate(
            flops=2 * count * rows * columns * width,
            bytes_accessed=6 * rows * width,
            transcendentals=rows,
        ),
        name="normed_back",
    )(qkv_grad, project_in, tokens)


def local(
    tokens,
    cotangent,
    routes,
    slot_index,
    first_gain,
    first_shift,
    project_in,
    project_out,
    second_gain,
    second_shift,
    router_weight,
    mixing_weight,
    dense_up,
    dense_down,
    expert_up,
    expert_down,
):
    row_count, width = tokens.shape
    expert_count = router_weight.shape[1]
    capacity = 2 * row_count // expert_count
    held = expert_up.shape[0]
    blocks = expert_count // held
    slot_total = expert_count * capacity
    head_columns = project_in.shape[2]
    parts = lax.axis_size("tensor")
    part_rows = row_count // parts
    my_start = lax.axis_index("tensor") * part_rows

    def mine(rows, axis=0):
        return lax.dynamic_slice_in_dim(rows, my_start, part_rows, axis)

    half = head_columns // 2
    odd = lax.axis_index("expert") % 2
    own_half = lax.all_gather(
        lax.dynamic_slice_in_dim(project_out, odd * half, half, 0), "tensor", axis=0
    )
    project_in = jnp.swapaxes(project_in, 0, 1)
    unit_in, _ = norm_stats(tokens.astype(F32))
    normed_low = (unit_in * first_gain + first_shift).astype(BF)
    qkv = jnp.einsum("td,cdn->ctn", normed_low, project_in, preferred_element_type=F32).astype(BF)
    attended, log_total = attend_forward(qkv)
    attended, own_half = lax.optimization_barrier((attended, own_half))
    attended_all = lax.all_gather(attended, "tensor", axis=0, tiled=True).reshape(
        parts, row_count, head_columns
    )

    swap = [(i, i ^ 1) for i in range(lax.axis_size("expert"))]
    other_half = lax.ppermute(own_half, "expert", swap)
    project_out_all = jnp.concatenate(
        [
            jnp.where(odd == 0, own_half, other_half),
            jnp.where(odd == 0, other_half, own_half),
        ],
        axis=1,
    )

    slot_place = jnp.where(slot_index < capacity, routes * capacity + slot_index, slot_total)
    slot_place = after(slot_place, attended)
    hit = lax.iota(jnp.int32, slot_total)[:, None] == slot_place[None, :]
    pick = hit.astype(BF)

    def to_slots(rows):
        return dot(pick, rows).astype(BF).reshape(blocks, held * capacity, width)

    def exchange(buffer):
        return lax.all_to_all(buffer, "expert", 0, 0, tiled=True)

    def from_slots(buffer):
        return t_dot(pick, buffer.reshape(slot_total, width))

    cotan_slots = exchange(to_slots(cotangent)).reshape(blocks, held, capacity, width)

    residual, mid_low = project_norm(
        attended_all, project_out_all, tokens, second_gain, second_shift
    )
    mid_slots = after(to_slots(mid_low), cotan_slots)
    arrived = exchange(mid_slots).reshape(blocks, held, capacity, width)
    mid_low = after(mid_low, mid_slots)
    router_logits = dot(mid_low, router_weight)
    mixing_logits = dot(mid_low, mixing_weight)
    router_probs = jax.nn.softmax(router_logits, axis=-1)
    mixing = jax.nn.softmax(mixing_logits, axis=-1)
    chosen = (routes[:, None] == lax.iota(jnp.int32, expert_count)[None, :]).astype(F32)
    gate = jnp.sum(chosen * router_probs, axis=-1, keepdims=True)
    dense_weight = mixing[:, 0:1]
    expert_weight = mixing[:, 1:2] * gate
    cotan = cotangent.astype(F32)

    dense_hidden, dense_slope = gelu_both(dot(mid_low, dense_up))
    dense_hidden = dense_hidden.astype(BF)
    dense_part = dot(dense_hidden, dense_down)
    dense_out_grad = (cotan * dense_weight).astype(BF)
    dense_pre_grad = (dot_t(dense_out_grad, dense_down) * dense_slope).astype(BF)
    mid_dense_part = dot_t(dense_pre_grad, dense_up)
    dense_down_grad = t_dot(dense_hidden, dense_out_grad)
    dense_up_grad = t_dot(mid_low, dense_pre_grad)
    dense_dot = jnp.sum(cotan * dense_part, axis=-1, keepdims=True)

    hidden_grads = expert_hidden_grad(after(cotan_slots, mid_slots), expert_down)
    hiddens, pre_grads, in_slots, slot_dots = expert_back(arrived, expert_up, hidden_grads)
    in_slots = in_slots.reshape(blocks, held * capacity, width)
    in_home = exchange(in_slots)

    slot_dot = jnp.swapaxes(slot_dots[:, :, 0].reshape(held, blocks, capacity), 0, 1)
    slot_dot = exchange(after(slot_dot.reshape(blocks, held * capacity), in_slots))
    slot_dot = slot_dot.reshape(slot_total)
    slot_weight = jnp.sum(jnp.where(hit, expert_weight[:, 0][None, :], 0.0), axis=1)
    slot_weight = exchange(after(slot_weight, slot_dot).reshape(blocks, held * capacity))
    slot_weight = slot_weight.reshape(blocks, held, capacity)
    out_slots = expert_down_rows(after(hiddens, in_slots), expert_down, blocks).reshape(
        blocks, held * capacity, width
    )
    out_home = exchange(after(out_slots, in_home))

    expert_dot = jnp.sum(jnp.where(hit, slot_dot[:, None], 0.0), axis=0)[:, None]
    gated_dot = gate * expert_dot
    mean_dot = dense_weight * dense_dot + mixing[:, 1:2] * gated_dot
    mixing_low = (mixing * (jnp.concatenate([dense_dot, gated_dot], axis=1) - mean_dot)).astype(BF)
    router_low = (expert_weight * expert_dot * (chosen - router_probs)).astype(BF)
    mid_part = (
        mid_dense_part
        + dot_t(router_low, router_weight)
        + dot_t(mixing_low, mixing_weight)
        + expert_weight * from_slots(in_home)
    )
    mid_low_part = mid_part.astype(BF)
    mid_grad = lax.psum_scatter(mid_low_part, "tensor", scatter_dimension=0, tiled=True)

    up_grads, down_grads = [], []
    for e in range(held):
        row_weight = after(slot_weight, in_home)[:, e].reshape(blocks * capacity, 1)
        grads = cotan_slots[:, e].reshape(blocks * capacity, width)
        rows = arrived[:, e].reshape(blocks * capacity, width)
        down_grads.append(t_dot(hiddens[e], (grads.astype(F32) * row_weight).astype(BF)))
        up_grads.append(t_dot(rows, (pre_grads[e].astype(F32) * row_weight).astype(BF)))
    expert_up_grad = jnp.stack(up_grads)
    expert_down_grad = jnp.stack(down_grads)
    out_part = dense_weight * dense_part + expert_weight * from_slots(after(out_home, mid_low_part))
    out_low = out_part.astype(BF)
    out_sum = lax.psum_scatter(
        after(out_low, mid_grad), "tensor", scatter_dimension=0, tiled=True
    )

    def pack(pieces):
        return jnp.concatenate([piece.reshape(blocks, -1, width) for piece in pieces], axis=1)

    def unpack(rows, sizes):
        starts = [sum(sizes[:i]) for i in range(len(sizes))]
        return [rows[..., s : s + n, :] for s, n in zip(starts, sizes)]

    mid_grad = mid_grad.astype(F32)
    residual_mine = mine(residual)
    unit_mine, inverse_mine = norm_stats(residual_mine)
    second_gain_grad = jnp.sum(mid_grad * unit_mine, axis=0)
    second_shift_grad = jnp.sum(mid_grad, axis=0)
    residual_grad = mine(cotangent).astype(F32) + norm_back(
        unit_mine, inverse_mine, second_gain, mid_grad
    )
    attn_grad_low = residual_grad.astype(BF)
    attended_grad = jnp.einsum(
        "td,znd->ztn", attn_grad_low, project_out_all, preferred_element_type=F32
    ).astype(BF)
    dense_sent = after(
        pack([dense_up_grad.astype(BF), dense_down_grad.astype(BF)]), out_home, attended_grad
    )
    attended_grad = lax.all_to_all(attended_grad, "tensor", 0, 0, tiled=True).reshape(
        row_count, head_columns
    )
    dense_got = exchange(dense_sent)
    qkv_grad = attend_backward(qkv, log_total, attended_grad)
    normed_low_part, first_sums = normed_back(qkv_grad, project_in, tokens)
    normed_grad = lax.psum_scatter(
        after(normed_low_part, out_sum), "tensor", scatter_dimension=0, tiled=True
    )
    late_residual, late_sum = lax.optimization_barrier(
        (residual, out_sum, normed_low_part)
    )[:2]
    layer_mine = (mine(late_residual) + late_sum.astype(F32)).astype(BF)
    normed_grad_f32 = normed_grad.astype(F32)
    unit_first, inverse_first = norm_stats(mine(tokens).astype(F32))
    input_mine = residual_grad + norm_back(unit_first, inverse_first, first_gain, normed_grad_f32)
    both_mine = jnp.stack([layer_mine, input_mine.astype(BF)])

    project_out_grad = jnp.einsum(
        "ztn,td->znd", mine(attended_all, 1), attn_grad_low, preferred_element_type=F32
    ).astype(BF)
    project_out_grad = jnp.swapaxes(
        project_out_grad.reshape(parts, blocks, head_columns // blocks, width), 0, 1
    ).reshape(parts * head_columns, width)
    project_in_grad = (
        jnp.einsum(
            "ctn,td->cnd", after(qkv_grad, normed_low_part), normed_low,
            preferred_element_type=F32,
        )
        .astype(BF)
        .reshape(3 * head_columns, width)
    )
    router_grad = t_dot(router_low, mid_low)
    mixing_grad = t_dot(mixing_low, mid_low)
    small = jnp.concatenate(
        [
            first_sums[:2],
            jnp.stack([second_gain_grad, second_shift_grad]),
            router_grad,
            mixing_grad,
        ],
        axis=0,
    )
    small_rows = small.shape[0]
    each = -(-small_rows // blocks)
    small = jnp.pad(small, ((0, each * blocks - small_rows), (0, 0))).reshape(blocks, each, width)
    small = jnp.pad(small, ((0, 0), (0, 16 - each), (0, 0))).astype(BF)
    rest_sent = pack([project_in_grad, project_out_grad, small.reshape(blocks * 16, width)])
    rest_got = exchange(after(rest_sent, dense_got))
    dense_got, rest_got, both_mine = lax.optimization_barrier((dense_got, rest_got, both_mine))
    both = lax.all_gather(both_mine, "tensor", axis=0)
    layer_out = both[:, 0].reshape(row_count, width)
    input_grad = both[:, 1].reshape(row_count, width)
    dense_piece = jnp.sum(dense_got.astype(F32), axis=0)
    project_in_piece, project_out_piece, small_piece = unpack(
        jnp.sum(rest_got.astype(F32), axis=0),
        [3 * head_columns // blocks, parts * head_columns // blocks, 16],
    )
    across = jnp.concatenate(
        [
            project_out_piece.reshape(parts, head_columns // blocks, width),
            jnp.broadcast_to(small_piece[None], (parts, 16, width)),
        ],
        axis=1,
    ).astype(BF)
    across = jnp.sum(
        lax.all_to_all(across, "tensor", 0, 0, tiled=True).astype(F32), axis=0
    )
    project_out_piece = across[: head_columns // blocks]
    small_piece = across[head_columns // blocks :]
    pieces = jnp.concatenate(
        [project_in_piece, project_out_piece, small_piece, dense_piece], axis=0
    ).astype(BF)
    sizes = [
        piece.shape[0] for piece in (project_in_piece, project_out_piece, small_piece)
    ] + [dense_piece.shape[0] // 2] * 2
    spread = exchange(jnp.broadcast_to(pieces[None], (blocks,) + pieces.shape))
    project_in_grad, project_out_grad, small, dense_up_grad, dense_down_grad = [
        piece.reshape(-1, width).astype(F32) for piece in unpack(spread, sizes)
    ]
    project_in_grad = jnp.transpose(project_in_grad.reshape(3, head_columns, width), (2, 0, 1))
    small = small.reshape(blocks, 16, width)[:, :each].reshape(blocks * each, width)

    return (
        layer_out,
        input_grad,
        small[0],
        small[1],
        project_in_grad,
        project_out_grad,
        small[2],
        small[3],
        small[4 : 4 + expert_count].T,
        small[4 + expert_count : 6 + expert_count].T,
        dense_up_grad,
        dense_down_grad,
        expert_up_grad,
        expert_down_grad,
    )


def solution(mesh):
    placed = (
        P("expert", None),
        P("expert", None),
        P("expert"),
        P("expert"),
        P(),
        P(),
        P(None, None, "tensor"),
        P("tensor", None),
        P(),
        P(),
        P(),
        P(),
        P(None, "tensor"),
        P("tensor", None),
        P("expert", None, "tensor"),
        P("expert", "tensor", None),
    )
    return jax.shard_map(
        local,
        mesh=mesh,
        in_specs=placed,
        out_specs=(
            P("expert", None),
            P("expert", None),
            P(),
            P(),
            P(None, None, "tensor"),
            P("tensor", None),
            P(),
            P(),
            P(),
            P(),
            P(None, "tensor"),
            P("tensor", None),
            P("expert", None, "tensor"),
            P("expert", "tensor", None),
        ),
        check_vma=False,
    )
```

```python
import functools

import jax
import jax.numpy as jnp
from jax import lax
from jax.experimental import pallas as pl
from jax.experimental.pallas import tpu as pltpu
from jax.sharding import PartitionSpec as P

HEAD_DIM = 64
EPS = 1e-05
NEGATIVE = -1e30
BF = jnp.bfloat16
F32 = jnp.float32


def norm_stats(rows):
    row_mean = jnp.mean(rows, axis=-1, keepdims=True)
    centred = rows - row_mean
    spread = jnp.mean(centred * centred, axis=-1, keepdims=True)
    inverse = lax.rsqrt(spread + EPS)
    return centred * inverse, inverse


def norm_back(unit, inverse, gain, grad):
    weighted = grad * gain
    first = jnp.mean(weighted, axis=-1, keepdims=True)
    second = jnp.mean(weighted * unit, axis=-1, keepdims=True)
    return inverse * (weighted - first - unit * second)


def gelu_both(v):
    square = v * v
    half = 0.5 + 0.5 * jnp.tanh(v * (0.7978845608 + 0.7978845608 * 0.044715 * square))
    steep = v * (1.5957691216 + 1.5957691216 * 0.134145 * square)
    return v * half, half + half * (steep * (1.0 - half))


def t_dot(a, b):
    return lax.dot_general(a, b, (((0,), (0,)), ((), ())), preferred_element_type=F32)


def after(value, *others):
    return lax.optimization_barrier((value,) + others)[0]


def dot(a, b):
    return jnp.dot(a, b, preferred_element_type=F32)

def dot_t(a, b):
    return lax.dot_general(a, b, (((1,), (1,)), ((), ())), preferred_element_type=F32)

def head_lanes(head, rows):
    lanes = lax.broadcasted_iota(jnp.int32, (rows, 2 * HEAD_DIM), 1)
    return (lanes < HEAD_DIM) if head == 0 else (lanes >= HEAD_DIM)

def keep_causal(scores, tile):
    keys = scores.shape[0]
    key_pos = lax.broadcasted_iota(jnp.int32, (tile, tile), 0)
    query_pos = lax.broadcasted_iota(jnp.int32, (tile, tile), 1)
    last = jnp.where(key_pos <= query_pos, scores[keys - tile :], NEGATIVE)
    if keys == tile:
        return last
    return jnp.concatenate([scores[: keys - tile], last], axis=0)

def attend_forward_kernel(tile, qkv_ref, out_ref, log_ref):
    rows = qkv_ref.shape[1]
    values_t = jnp.transpose(qkv_ref[2])
    for block in range(rows // tile):
        keys = (block + 1) * tile
        here = pl.ds(block * tile, tile)
        query_block = qkv_ref[0, here, :]
        pieces, logs = [], []
        for head in range(2):
            q = jnp.where(head_lanes(head, tile), query_block, jnp.zeros_like(query_block))
            scores = dot_t(qkv_ref[1, :keys, :], q) * (HEAD_DIM ** (-0.5))
            scores = keep_causal(scores, tile)
            top = jnp.max(scores, axis=0, keepdims=True)
            powers = jnp.exp(scores - top)
            total = jnp.sum(powers, axis=0, keepdims=True)
            blended = dot(values_t[head * HEAD_DIM : (head + 1) * HEAD_DIM, :keys], powers.astype(BF))
            pieces.append(blended / total)
            logs.append(top + jnp.log(total))
        out_ref[here, :] = jnp.transpose(jnp.concatenate(pieces, axis=0)).astype(BF)
        for head in range(2):
            log_ref[0, head : head + 1, here] = logs[head]

def attend_backward_kernel(tile, qkv_ref, log_ref, grad_ref, out_ref, key_acc, value_acc):
    rows = qkv_ref.shape[1]
    scale = HEAD_DIM ** (-0.5)
    keys_t = jnp.transpose(qkv_ref[1])
    count = rows // tile
    for block in reversed(range(count)):
        keys = (block + 1) * tile
        here = pl.ds(block * tile, tile)
        query_block = qkv_ref[0, here, :]
        grad_block = grad_ref[here, :]
        pieces = []
        for head in range(2):
            lanes = head_lanes(head, tile)
            q = jnp.where(lanes, query_block, jnp.zeros_like(query_block))
            g = jnp.where(lanes, grad_block, jnp.zeros_like(grad_block))
            scores = dot_t(qkv_ref[1, :keys, :], q) * scale
            scores = keep_causal(scores, tile)
            weights = jnp.exp(scores - log_ref[0, head : head + 1, here])
            weight_grad = dot_t(qkv_ref[2, :keys, :], g)
            inner = jnp.sum(weights * weight_grad, axis=0, keepdims=True)
            score_grad = (weights * (weight_grad - inner)).astype(BF)
            key_step = dot(score_grad, q)
            value_step = dot(weights.astype(BF), g)
            if block == count - 1 and head == 0:
                key_acc[...] = key_step
                value_acc[...] = value_step
            else:
                key_acc[:keys, :] += key_step
                value_acc[:keys, :] += value_step
            pieces.append(dot(keys_t[head * HEAD_DIM : (head + 1) * HEAD_DIM, :keys], score_grad))
        out_ref[0, here, :] = (jnp.transpose(jnp.concatenate(pieces, axis=0)) * scale).astype(BF)
    out_ref[1] = (key_acc[...] * scale).astype(BF)
    out_ref[2] = value_acc[...].astype(BF)

def attend_forward(qkv, tile=256):
    _, rows, columns = qkv.shape
    pairs = columns // (2 * HEAD_DIM)
    return pl.pallas_call(
        functools.partial(attend_forward_kernel, tile),
        grid=(pairs,),
        out_shape=(
            jax.ShapeDtypeStruct((rows, columns), BF),
            jax.ShapeDtypeStruct((pairs, 8, rows), F32),
        ),
        in_specs=[pl.BlockSpec((3, rows, 2 * HEAD_DIM), lambda p: (0, 0, p))],
        out_specs=(
            pl.BlockSpec((rows, 2 * HEAD_DIM), lambda p: (0, p)),
            pl.BlockSpec((1, 8, rows), lambda p: (p, 0, 0)),
        ),
        cost_estimate=pl.CostEstimate(
            flops=8 * rows * rows * columns // 2, bytes_accessed=8 * rows * columns,
            transcendentals=rows * rows * columns // 128),
        name="attend_forward",
    )(qkv)

def attend_backward(qkv, logs, grads, tile=256):
    _, rows, columns = qkv.shape
    pairs = columns // (2 * HEAD_DIM)
    return pl.pallas_call(
        functools.partial(attend_backward_kernel, tile),
        grid=(pairs,),
        out_shape=jax.ShapeDtypeStruct((3, rows, columns), BF),
        in_specs=[
            pl.BlockSpec((3, rows, 2 * HEAD_DIM), lambda p: (0, 0, p)),
            pl.BlockSpec((1, 8, rows), lambda p: (p, 0, 0)),
            pl.BlockSpec((rows, 2 * HEAD_DIM), lambda p: (0, p)),
        ],
        out_specs=pl.BlockSpec((3, rows, 2 * HEAD_DIM), lambda p: (0, 0, p)),
        scratch_shapes=[pltpu.VMEM((rows, 2 * HEAD_DIM), F32)] * 2,
        cost_estimate=pl.CostEstimate(
            flops=20 * rows * rows * columns // 2, bytes_accessed=16 * rows * columns,
            transcendentals=rows * rows * columns // 128),
        name="attend_backward",
    )(qkv, logs, grads)


def project_kernel(heads_ref, weight_ref, token_ref, gain_ref, shift_ref, rest_ref, low_ref):
    total = token_ref[...].astype(F32)
    for z in range(heads_ref.shape[0]):
        total = total + dot(heads_ref[z], weight_ref[z])
    rest_ref[...] = total
    unit, _ = norm_stats(total)
    low_ref[...] = (unit * gain_ref[...] + shift_ref[...]).astype(BF)


def project_norm(heads, weight, tokens, gain, shift, tile=256):
    parts, rows, columns = heads.shape
    width = weight.shape[2]
    block = lambda i: (i, 0)
    return pl.pallas_call(
        project_kernel,
        grid=(rows // tile,),
        out_shape=(
            jax.ShapeDtypeStruct((rows, width), F32),
            jax.ShapeDtypeStruct((rows, width), BF),
        ),
        in_specs=[
            pl.BlockSpec((parts, tile, columns), lambda i: (0, i, 0)),
            pl.BlockSpec((parts, columns, width), lambda i: (0, 0, 0)),
            pl.BlockSpec((tile, width), block),
            pl.BlockSpec((1, width), lambda i: (0, 0)),
            pl.BlockSpec((1, width), lambda i: (0, 0)),
        ],
        out_specs=(pl.BlockSpec((tile, width), block), pl.BlockSpec((tile, width), block)),
        cost_estimate=pl.CostEstimate(
            flops=2 * rows * parts * columns * width,
            bytes_accessed=12 * rows * width,
            transcendentals=rows,
        ),
        name="project_norm",
    )(heads, weight, tokens, gain[None], shift[None])


def gelu_back_kernel(rows_ref, up_ref, hidden_grad_ref, hidden_ref, pre_grad_ref, in_ref, dot_ref):
    shape = rows_ref.shape
    count = shape[0] * shape[2]
    rows = rows_ref[...].reshape(count, shape[3])
    units = up_ref.shape[2]
    step = min(256, units)
    dots = None
    for start in range(0, units, step):
        here = slice(start, start + step)
        hidden, slope = gelu_both(dot(rows, up_ref[0, :, here]))
        hidden = hidden.astype(BF)
        hidden_ref[0, :, here] = hidden
        hidden_grad = hidden_grad_ref[0, :, here].astype(F32)
        pre_grad_ref[0, :, here] = (hidden_grad * slope).astype(BF)
        product = hidden.astype(F32) * hidden_grad
        for lane in range(0, step, 128):
            part = product[:, lane : lane + 128]
            dots = part if dots is None else dots + part
    columns = in_ref.shape[3]
    in_ref[...] = dot_t(pre_grad_ref[0], up_ref[0, :columns, :]).astype(BF).reshape(in_ref.shape)
    capacity = shape[2]
    for block in range(shape[0]):
        here = jnp.transpose(dots[block * capacity : (block + 1) * capacity])
        here = jnp.sum(here, axis=0, keepdims=True)
        dot_ref[0, block] = jnp.broadcast_to(here, (8, capacity))


def expert_back(arrived, expert_up, hidden_grads, tile=512):
    blocks, held, capacity, width = arrived.shape
    rows = blocks * capacity
    units = expert_up.shape[2]
    slots = lambda e, i: (i, e, 0, 0)
    flat = pl.BlockSpec((1, tile, units), lambda e, i: (e, i, 0))
    return pl.pallas_call(
        gelu_back_kernel,
        grid=(held, rows // tile),
        out_shape=(
            jax.ShapeDtypeStruct((held, rows, units), BF),
            jax.ShapeDtypeStruct((held, rows, units), BF),
            jax.ShapeDtypeStruct((blocks, held, capacity, width // 2), BF),
            jax.ShapeDtypeStruct((held, blocks, 8, capacity), F32),
        ),
        in_specs=[
            pl.BlockSpec((tile // capacity, 1, capacity, width), slots),
            pl.BlockSpec((1, width, units), lambda e, i: (e, 0, 0)),
            flat,
        ],
        out_specs=(
            flat,
            flat,
            pl.BlockSpec((tile // capacity, 1, capacity, width // 2), slots),
            pl.BlockSpec((1, tile // capacity, 8, capacity), lambda e, i: (e, i, 0, 0)),
        ),
        cost_estimate=pl.CostEstimate(
            flops=3 * held * rows * units * width,
            bytes_accessed=13 * held * rows * width,
            transcendentals=held * rows * units,
        ),
        name="expert_back",
    )(arrived, expert_up, hidden_grads)


EXTRA = 16


def slot_tail_kernel(flat_ref, weight_ref, dot_ref, out_ref):
    count, _, size, columns = out_ref.shape
    capacity = size - EXTRA
    rows = dot_t(flat_ref[0], weight_ref[0]).astype(BF)
    for block in range(count):
        out_ref[block, 0, :capacity, :] = rows[block * capacity : (block + 1) * capacity]
        dots = dot_ref[0, block]
        low = dots - dots.astype(BF).astype(F32)
        line = lax.broadcasted_iota(jnp.int32, dots.shape, 0)
        both = jnp.where(line == 0, dots, jnp.where(line == 1, low, 0.0))
        out_ref[block, 0, capacity:, :] = jnp.zeros((EXTRA, columns), BF)
        out_ref[block, 0, capacity:, :capacity] = jnp.concatenate(
            [both, jnp.zeros_like(both)], axis=0
        ).astype(BF)


def slot_tail_rows(flat, weight, dots, columns, tile=512):
    held, rows, depth = flat.shape
    _, blocks, _, capacity = dots.shape
    return pl.pallas_call(
        slot_tail_kernel,
        grid=(held, rows // tile),
        out_shape=jax.ShapeDtypeStruct((blocks, held, capacity + EXTRA, columns), BF),
        in_specs=[
            pl.BlockSpec((1, tile, depth), lambda e, i: (e, i, 0)),
            pl.BlockSpec((1, columns, depth), lambda e, i: (e, 1, 0)),
            pl.BlockSpec((1, tile // capacity, 8, capacity), lambda e, i: (e, i, 0, 0)),
        ],
        out_specs=pl.BlockSpec(
            (tile // capacity, 1, capacity + EXTRA, columns), lambda e, i: (i, e, 0, 0)
        ),
        cost_estimate=pl.CostEstimate(
            flops=2 * held * rows * depth * columns,
            bytes_accessed=4 * held * rows * (depth + columns),
            transcendentals=0,
        ),
        name="slot_tail_rows",
    )(flat, weight, dots)


def slot_rows_kernel(flat_ref, weight_ref, out_ref):
    out_ref[...] = dot(flat_ref[0], weight_ref[0]).astype(BF).reshape(out_ref.shape)


def slot_rows(flat, weight, part, columns, blocks, tile=512):
    held, rows, depth = flat.shape
    capacity = rows // blocks
    return pl.pallas_call(
        slot_rows_kernel,
        grid=(held, rows // tile),
        out_shape=jax.ShapeDtypeStruct((blocks, held, capacity, columns), BF),
        in_specs=[
            pl.BlockSpec((1, tile, depth), lambda e, i: (e, i, 0)),
            pl.BlockSpec((1, depth, columns), lambda e, i: (e, 0, part)),
        ],
        out_specs=pl.BlockSpec(
            (tile // capacity, 1, capacity, columns), lambda e, i: (i, e, 0, 0)
        ),
        cost_estimate=pl.CostEstimate(
            flops=2 * held * rows * depth * columns,
            bytes_accessed=4 * held * rows * (depth + columns),
            transcendentals=0,
        ),
        name="slot_rows",
    )(flat, weight)


def combine_kernel(place_ref, weight_ref, back_ref, base_ref, out_ref):
    tile, slots = place_ref.shape[0], back_ref.shape[0]
    pick = lax.broadcasted_iota(jnp.int32, (tile, slots), 1) == place_ref[...]
    rows = dot(pick.astype(BF), back_ref[...])
    out_ref[...] = (base_ref[...] + weight_ref[...] * rows).astype(BF)


def combine(place, weight, back, base, part, tile=256):
    slots, columns = back.shape
    rows = base.shape[0]
    own = pl.BlockSpec((tile, 1), lambda i: (i, 0))
    return pl.pallas_call(
        combine_kernel,
        grid=(rows // tile,),
        out_shape=jax.ShapeDtypeStruct((rows, columns), BF),
        in_specs=[
            own,
            own,
            pl.BlockSpec((slots, columns), lambda i: (0, 0)),
            pl.BlockSpec((tile, columns), lambda i: (i, part)),
        ],
        out_specs=pl.BlockSpec((tile, columns), lambda i: (i, 0)),
        cost_estimate=pl.CostEstimate(
            flops=2 * rows * slots * columns,
            bytes_accessed=2 * slots * columns + 6 * rows * columns,
            transcendentals=0,
        ),
        name="combine",
    )(place, weight, back, base)


def hidden_grad_kernel(grads_ref, down_ref, out_ref):
    shape = grads_ref.shape
    rows = grads_ref[...].reshape(shape[0] * shape[2], shape[3])
    out_ref[0] = dot_t(rows, down_ref[0]).astype(BF)


def expert_hidden_grad(cotan_slots, expert_down, tile=512):
    blocks, held, capacity, width = cotan_slots.shape
    rows = blocks * capacity
    units = expert_down.shape[1]
    return pl.pallas_call(
        hidden_grad_kernel,
        grid=(held, rows // tile),
        out_shape=jax.ShapeDtypeStruct((held, rows, units), BF),
        in_specs=[
            pl.BlockSpec((tile // capacity, 1, capacity, width), lambda e, i: (i, e, 0, 0)),
            pl.BlockSpec((1, units, width), lambda e, i: (e, 0, 0)),
        ],
        out_specs=pl.BlockSpec((1, tile, units), lambda e, i: (e, i, 0)),
        cost_estimate=pl.CostEstimate(
            flops=2 * held * rows * units * width,
            bytes_accessed=6 * held * rows * width,
            transcendentals=0,
        ),
        name="expert_hidden_grad",
    )(cotan_slots, expert_down)


def normed_kernel(grad_ref, weight_ref, token_ref, out_ref, sums_ref):
    total = dot_t(grad_ref[0], weight_ref[0])
    for c in range(1, grad_ref.shape[0]):
        total = total + dot_t(grad_ref[c], weight_ref[c])
    out_ref[...] = total.astype(BF)
    unit, _ = norm_stats(token_ref[...].astype(F32))

    @pl.when(pl.program_id(0) == 0)
    def _():
        sums_ref[...] = jnp.zeros_like(sums_ref)

    sums_ref[0:1, :] += jnp.sum(total * unit, axis=0, keepdims=True)
    sums_ref[1:2, :] += jnp.sum(total, axis=0, keepdims=True)


def normed_back(qkv_grad, project_in, tokens, tile=256):
    count, rows, columns = qkv_grad.shape
    width = project_in.shape[1]
    return pl.pallas_call(
        normed_kernel,
        grid=(rows // tile,),
        out_shape=(
            jax.ShapeDtypeStruct((rows, width), BF),
            jax.ShapeDtypeStruct((8, width), F32),
        ),
        in_specs=[
            pl.BlockSpec((count, tile, columns), lambda i: (0, i, 0)),
            pl.BlockSpec((count, width, columns), lambda i: (0, 0, 0)),
            pl.BlockSpec((tile, width), lambda i: (i, 0)),
        ],
        out_specs=(
            pl.BlockSpec((tile, width), lambda i: (i, 0)),
            pl.BlockSpec((8, width), lambda i: (0, 0)),
        ),
        cost_estimate=pl.CostEstimate(
            flops=2 * count * rows * columns * width,
            bytes_accessed=6 * rows * width,
            transcendentals=rows,
        ),
        name="normed_back",
    )(qkv_grad, project_in, tokens)


def mid_back_kernel(
    place_ref, low_half_ref, high_half_ref, gates_ref, rest_ref, cotan_ref, gain_ref, weight_ref,
    heads_ref, rest_grad_ref, low_ref, sums_ref,
):
    grad = jnp.concatenate([low_half_ref[...], high_half_ref[...]], axis=1).astype(F32)
    grad = grad + gates_ref[...]
    unit, inverse = norm_stats(rest_ref[...])
    rest_grad = cotan_ref[...].astype(F32) + norm_back(unit, inverse, gain_ref[...], grad)
    rest_grad_ref[...] = rest_grad
    low = rest_grad.astype(BF)
    low_ref[...] = low
    for z in range(weight_ref.shape[0]):
        heads_ref[z] = dot_t(low, weight_ref[z]).astype(BF)
    sums_ref[0:1, :] = jnp.sum(grad * unit, axis=0, keepdims=True)
    sums_ref[1:2, :] = jnp.sum(grad, axis=0, keepdims=True)


def mid_back(place, mid_grads, gates, residual, cotangent, gain, weight):
    parts, columns, width = weight.shape
    rows = mid_grads[0].shape[0]
    here = lambda i, place: (place[0], 0)
    whole = lambda i, place: (0, 0)
    cube = lambda i, place: (0, 0, 0)
    return pl.pallas_call(
        mid_back_kernel,
        grid_spec=pltpu.PrefetchScalarGridSpec(
            num_scalar_prefetch=1,
            grid=(1,),
            in_specs=[
                pl.BlockSpec((rows, width // 2), whole),
                pl.BlockSpec((rows, width // 2), whole),
                pl.BlockSpec((rows, width), whole),
                pl.BlockSpec((rows, width), here),
                pl.BlockSpec((rows, width), here),
                pl.BlockSpec((1, width), whole),
                pl.BlockSpec((parts, columns, width), cube),
            ],
            out_specs=(
                pl.BlockSpec((parts, rows, columns), cube),
                pl.BlockSpec((rows, width), whole),
                pl.BlockSpec((rows, width), whole),
                pl.BlockSpec((8, width), whole),
            ),
        ),
        out_shape=(
            jax.ShapeDtypeStruct((parts, rows, columns), BF),
            jax.ShapeDtypeStruct((rows, width), F32),
            jax.ShapeDtypeStruct((rows, width), BF),
            jax.ShapeDtypeStruct((8, width), F32),
        ),
        cost_estimate=pl.CostEstimate(
            flops=2 * rows * parts * columns * width,
            bytes_accessed=16 * rows * width,
            transcendentals=rows,
        ),
        name="mid_back",
    )(place[None], *mid_grads, gates, residual, cotangent, gain[None], weight)


def local(
    tokens,
    cotangent,
    routes,
    slot_index,
    first_gain,
    first_shift,
    project_in,
    project_out,
    second_gain,
    second_shift,
    router_weight,
    mixing_weight,
    dense_up,
    dense_down,
    expert_up,
    expert_down,
):
    row_count, width = tokens.shape
    expert_count = router_weight.shape[1]
    capacity = 2 * row_count // expert_count
    held = expert_up.shape[0]
    blocks = expert_count // held
    slot_total = expert_count * capacity
    head_columns = project_in.shape[2]
    parts = lax.axis_size("tensor")
    part_rows = row_count // parts
    my_start = lax.axis_index("tensor") * part_rows

    def mine(rows, axis=0):
        return lax.dynamic_slice_in_dim(rows, my_start, part_rows, axis)

    z = lax.axis_index("tensor")

    def shift_tensor(pick):
        return [
            lax.ppermute(pick(k), "tensor", [(i, (i + k) % parts) for i in range(parts)])
            if k
            else pick(0)
            for k in range(parts)
        ]

    def scatter_tensor(rows):
        return shift_tensor(
            lambda k: lax.dynamic_index_in_dim(rows, (z + k) % parts, 0, keepdims=False)
        )

    def in_order(pieces):
        twice = jnp.stack(pieces[::-1] * 2)
        return lax.dynamic_slice_in_dim(twice, parts - 1 - z, parts, 0)

    place = lax.axis_index("expert")
    odd = place % 2
    far = place // 2 % 2
    quarter = head_columns // 4
    own = lax.dynamic_slice_in_dim(project_out, (2 * far + odd) * quarter, quarter, 0)
    own = lax.all_to_all(
        jnp.broadcast_to(own[None], (parts,) + own.shape), "tensor", 0, 0, tiled=True
    )
    project_in = jnp.swapaxes(project_in, 0, 1)
    unit_in, _ = norm_stats(tokens.astype(F32))
    normed_low = (unit_in * first_gain + first_shift).astype(BF)
    qkv = jnp.einsum("td,cdn->ctn", normed_low, project_in, preferred_element_type=F32).astype(BF)
    attended, log_total = attend_forward(qkv)
    attended_all = lax.all_gather(attended, "tensor", axis=0, tiled=True).reshape(
        parts, row_count, head_columns
    )
    pairs = [(i, i ^ 1) for i in range(blocks)]

    def from_pair(rows):
        return lax.ppermute(rows, "expert", pairs)

    def both_sides(side, own, other):
        return jnp.stack([jnp.where(side == 0, own, other), jnp.where(side == 0, other, own)])

    slot_place = jnp.where(slot_index < capacity, routes * capacity + slot_index, slot_total)
    slot_place = after(slot_place, attended)
    hit = lax.iota(jnp.int32, slot_total)[:, None] == slot_place[None, :]
    pick = hit.astype(BF)

    def to_slots(rows):
        return dot(pick, rows).astype(BF).reshape(blocks, held * capacity, width)

    def exchange(buffer):
        return lax.all_to_all(buffer, "expert", 0, 0, tiled=True)

    own_far = lax.ppermute(own, "expert", [(i, i ^ 2) for i in range(blocks)])
    cotan_sent, own_far = lax.optimization_barrier((to_slots(cotangent), own_far))
    cotan_slots = exchange(cotan_sent).reshape(blocks, held, capacity, width)
    own_sides = both_sides(far, own, own_far)
    project_out_all = jnp.transpose(both_sides(odd, own_sides, from_pair(own_sides)), (2, 1, 0, 3, 4))
    project_out_all = project_out_all.reshape(parts, head_columns, width)

    residual, mid_low = project_norm(
        attended_all, project_out_all, tokens, second_gain, second_shift
    )
    mid_slots = to_slots(mid_low)
    arrived = exchange(mid_slots).reshape(blocks, held, capacity, width)
    mid_low = after(mid_low, mid_slots, cotan_slots)
    router_logits = dot(mid_low, router_weight)
    mixing_logits = dot(mid_low, mixing_weight)
    router_probs = jax.nn.softmax(router_logits, axis=-1)
    mixing = jax.nn.softmax(mixing_logits, axis=-1)
    chosen = (routes[:, None] == lax.iota(jnp.int32, expert_count)[None, :]).astype(F32)
    gate = jnp.sum(chosen * router_probs, axis=-1, keepdims=True)
    dense_weight = mixing[:, 0:1]
    expert_weight = mixing[:, 1:2] * gate
    cotan = cotangent.astype(F32)

    dense_hidden, dense_slope = gelu_both(dot(mid_low, dense_up))
    dense_hidden = dense_hidden.astype(BF)
    dense_part = dot(dense_hidden, dense_down)
    dense_out_grad = (cotan * dense_weight).astype(BF)
    dense_pre_grad = (dot_t(dense_out_grad, dense_down) * dense_slope).astype(BF)
    mid_dense_part = dot_t(dense_pre_grad, dense_up)
    dense_down_grad = t_dot(dense_hidden, dense_out_grad)
    dense_up_grad = t_dot(mid_low, dense_pre_grad)
    dense_dot = jnp.sum(cotan * dense_part, axis=-1, keepdims=True)

    hidden_grads = expert_hidden_grad(after(cotan_slots, mid_slots), expert_down)
    slot_weight = jnp.sum(jnp.where(hit, expert_weight[:, 0][None, :], 0.0), axis=1)
    slot_weight = slot_weight.reshape(blocks, held * capacity)
    arrived, mid_dense_part, dense_dot, dense_up_grad, dense_down_grad = lax.optimization_barrier(
        (arrived, mid_dense_part, dense_dot, dense_up_grad, dense_down_grad)
    )
    hiddens, pre_grads, low_slots, slot_dots = expert_back(arrived, expert_up, hidden_grads)
    low_home = exchange(low_slots.reshape(blocks, held * capacity, width // 2))
    high_slots = slot_tail_rows(after(pre_grads, low_slots), expert_up, slot_dots, width // 2)
    out_slots = slot_rows(after(hiddens, high_slots), expert_down, 0, width, blocks)
    high_home = exchange(
        after(high_slots, out_slots).reshape(blocks, held * (capacity + EXTRA), width // 2)
    )
    high_home, out_slots = lax.optimization_barrier((high_home, out_slots))
    out_home = exchange(out_slots.reshape(blocks, held * capacity, width))

    out_base = dense_weight * dense_part
    place_column = slot_place[:, None]
    tail_column = jnp.where(
        slot_index < capacity, routes * (capacity + EXTRA) + slot_index,
        expert_count * (capacity + EXTRA),
    )[:, None]

    def sum_rows(rows):
        return lax.psum_scatter(rows, "tensor", scatter_dimension=0, tiled=True)

    mid_low_half = combine(
        place_column, expert_weight, low_home.reshape(slot_total, -1), mid_dense_part, 0
    )
    mid_high_half = combine(
        tail_column,
        expert_weight,
        high_home.reshape(expert_count * (capacity + EXTRA), -1),
        mid_dense_part,
        1,
    )
    mid_grad_low = sum_rows(mid_low_half)
    mid_grad_high = sum_rows(after(mid_high_half, mid_low_half))

    slot_dot = after(high_home, mid_high_half).reshape(
        blocks, held, capacity + EXTRA, width // 2
    )[:, :, capacity : capacity + 2, :capacity]
    slot_dot = jnp.sum(slot_dot.astype(F32), axis=2).reshape(slot_total)
    expert_dot = jnp.sum(jnp.where(hit, slot_dot[:, None], 0.0), axis=0)
    dots = jnp.stack([dense_dot[:, 0], expert_dot]).reshape(2, parts, part_rows)
    dots = sum(scatter_tensor(jnp.swapaxes(dots, 0, 1)))[:, :, None]
    dense_dot, expert_dot = dots[0], dots[1]
    gate_mine, mixing_mine = mine(gate), mine(mixing)
    gated_dot = gate_mine * expert_dot
    mean_dot = mixing_mine[:, 0:1] * dense_dot + mixing_mine[:, 1:2] * gated_dot
    mixing_low = (
        mixing_mine * (jnp.concatenate([dense_dot, gated_dot], axis=1) - mean_dot)
    ).astype(BF)
    router_low = (
        mixing_mine[:, 1:2] * gated_dot * (mine(chosen) - mine(router_probs))
    ).astype(BF)
    gates_mine = dot_t(router_low, router_weight) + dot_t(mixing_low, mixing_weight)

    chips = blocks // 2
    same_core = [[2 * i + core for i in range(chips)] for core in range(2)]

    def exchange_chips(buffer):
        return lax.all_to_all(
            buffer, "expert", 0, 0, tiled=True, axis_index_groups=same_core
        )

    def split(rows):
        return rows.reshape(2, chips, -1, width)

    def pair_sum(rows):
        sent = lax.dynamic_index_in_dim(rows, 1 - odd, 0, keepdims=False)
        kept = lax.dynamic_index_in_dim(rows, odd, 0, keepdims=False)
        return (kept.astype(F32) + from_pair(sent).astype(F32)).astype(BF)

    def spread(piece):
        got = exchange_chips(jnp.broadcast_to(piece[None], (chips,) + piece.shape))
        return got, from_pair(got)

    dense_half = pair_sum(
        jnp.concatenate([split(dense_up_grad.astype(BF)), split(dense_down_grad.astype(BF))], axis=2)
    )
    dense_got = exchange_chips(after(dense_half, out_home))

    attended_grad, residual_grad, attn_grad_low, second_sums = mid_back(
        lax.axis_index("tensor"),
        (mid_grad_low, mid_grad_high),
        gates_mine,
        residual,
        cotangent,
        second_gain,
        project_out_all,
    )
    attended_grad_sent = attended_grad
    out_sum = sum_rows(
        combine(
            place_column,
            expert_weight,
            after(out_home, attended_grad_sent).reshape(slot_total, -1),
            out_base,
            0,
        )
    )
    attended_grad = in_order(scatter_tensor(attended_grad)).reshape(row_count, head_columns)
    project_out_grad = jnp.einsum(
        "ztn,td->znd",
        mine(attended_all, 1),
        after(attn_grad_low, attended_grad_sent),
        preferred_element_type=F32,
    ).astype(BF)
    dense_piece = jnp.sum(after(dense_got, attended_grad_sent).astype(F32), axis=0).astype(BF)
    qkv_grad = attend_backward(qkv, log_total, attended_grad)
    normed_low_part, first_sums = normed_back(after(qkv_grad, dense_got), project_in, tokens)
    slot_weight = exchange(after(slot_weight, normed_low_part)).reshape(blocks, held, capacity)
    late_residual, late_sum = lax.optimization_barrier(
        (residual, out_sum, normed_low_part)
    )[:2]
    layer_mine = (mine(late_residual) + late_sum.astype(F32)).astype(BF)
    layer_out = lax.all_gather(layer_mine, "tensor", axis=0, tiled=True)
    normed_grad = lax.psum_scatter(
        after(normed_low_part, layer_mine), "tensor", scatter_dimension=0, tiled=True
    )
    project_in_grad = (
        jnp.einsum(
            "ctn,td->cnd", after(qkv_grad, normed_low_part), normed_low,
            preferred_element_type=F32,
        )
        .astype(BF)
        .reshape(3 * head_columns, width)
    )
    small = jnp.concatenate(
        [
            first_sums[:2],
            second_sums[:2],
            t_dot(after(router_low, attended_grad_sent), mine(mid_low)),
            t_dot(after(mixing_low, attended_grad_sent), mine(mid_low)),
        ],
        axis=0,
    )
    each = -(-small.shape[0] // blocks)
    small = jnp.pad(small, ((0, each * blocks - small.shape[0]), (0, 0)))
    small = jnp.pad(small.reshape(blocks, each, width), ((0, 0), (0, 16 - each), (0, 0)))
    out_rows = head_columns // blocks
    rest = jnp.concatenate(
        [
            split(project_in_grad),
            jnp.transpose(
                project_out_grad.reshape(parts, 2, chips, out_rows, width), (1, 2, 0, 3, 4)
            ).reshape(2, chips, parts * out_rows, width),
            split(small.astype(BF)),
        ],
        axis=2,
    )
    rest_half = pair_sum(rest)
    rest_got = exchange_chips(after(rest_half, dense_piece, slot_weight))
    rest_piece = jnp.sum(rest_got.astype(F32), axis=0).astype(BF)
    dense = exchange_chips(
        jnp.broadcast_to(after(dense_piece, rest_piece)[None], (chips,) + dense_piece.shape)
    )

    normed_grad = after(normed_grad, layer_out, rest_piece).astype(F32)
    unit_first, inverse_first = norm_stats(mine(tokens).astype(F32))
    input_mine = residual_grad + norm_back(unit_first, inverse_first, first_gain, normed_grad)
    input_mine = input_mine.astype(BF)
    up_grads, down_grads = [], []
    for e in range(held):
        row_weight = slot_weight[:, e].reshape(blocks * capacity, 1)
        down_weight = after(row_weight, rest_half)
        up_weight = after(row_weight, input_mine)
        grads = cotan_slots[:, e].reshape(blocks * capacity, width)
        rows = arrived[:, e].reshape(blocks * capacity, width)
        down_grads.append(t_dot(hiddens[e], (grads.astype(F32) * down_weight).astype(BF)))
        up_grads.append(t_dot(rows, (pre_grads[e].astype(F32) * up_weight).astype(BF)))
    expert_up_grad = jnp.stack(up_grads)
    expert_down_grad = jnp.stack(down_grads)
    input_grad = lax.all_gather(input_mine, "tensor", axis=0, tiled=True)

    in_rows = 3 * out_rows
    across = jnp.concatenate(
        [
            rest_piece[in_rows:-16].reshape(parts, out_rows, width),
            jnp.broadcast_to(rest_piece[None, -16:], (parts, 16, width)),
        ],
        axis=1,
    )
    across = after(scatter_tensor(across), input_mine)
    across = sum(piece.astype(F32) for piece in across).astype(BF)
    dense = after(dense, input_mine)
    dense_other = from_pair(dense)
    rest, rest_other = spread(jnp.concatenate([rest_piece[:in_rows], across], axis=0))
    rest = both_sides(odd, rest, rest_other).reshape(blocks, -1, width)
    dense = both_sides(odd, dense, dense_other).reshape(blocks, 2, -1, width)
    dense_up_grad = dense[:, 0].astype(F32).reshape(width, width)
    dense_down_grad = dense[:, 1].astype(F32).reshape(width, width)
    project_in_grad = rest[:, :in_rows].astype(F32).reshape(3, head_columns, width)
    project_in_grad = jnp.transpose(project_in_grad, (2, 0, 1))
    project_out_grad = rest[:, in_rows:-16].astype(F32).reshape(head_columns, width)
    small = rest[:, -16:][:, :each].astype(F32).reshape(blocks * each, width)

    return (
        layer_out,
        input_grad,
        small[0],
        small[1],
        project_in_grad,
        project_out_grad,
        small[2],
        small[3],
        small[4 : 4 + expert_count].T,
        small[4 + expert_count : 6 + expert_count].T,
        dense_up_grad,
        dense_down_grad,
        expert_up_grad,
        expert_down_grad,
    )


def solution(mesh):
    placed = (
        P("expert", None),
        P("expert", None),
        P("expert"),
        P("expert"),
        P(),
        P(),
        P(None, None, "tensor"),
        P("tensor", None),
        P(),
        P(),
        P(),
        P(),
        P(None, "tensor"),
        P("tensor", None),
        P("expert", None, "tensor"),
        P("expert", "tensor", None),
    )
    return jax.shard_map(
        local,
        mesh=mesh,
        in_specs=placed,
        out_specs=(
            P("expert", None),
            P("expert", None),
            P(),
            P(),
            P(None, None, "tensor"),
            P("tensor", None),
            P(),
            P(),
            P(),
            P(),
            P(None, "tensor"),
            P("tensor", None),
            P("expert", None, "tensor"),
            P("expert", "tensor", None),
        ),
        check_vma=False,
    )
```

```python
import functools

import jax
import jax.numpy as jnp
from jax import lax
from jax.experimental import pallas as pl
from jax.experimental.pallas import tpu as pltpu
from jax.sharding import PartitionSpec as P

HEAD_DIM = 64
EPS = 1e-05
NEGATIVE = -1e30
EXTRA = 8
BF = jnp.bfloat16
F32 = jnp.float32


def norm_stats(rows):
    row_mean = jnp.mean(rows, axis=-1, keepdims=True)
    centred = rows - row_mean
    spread = jnp.mean(centred * centred, axis=-1, keepdims=True)
    inverse = lax.rsqrt(spread + EPS)
    return centred * inverse, inverse


def norm_back(unit, inverse, gain, grad):
    weighted = grad * gain
    first = jnp.mean(weighted, axis=-1, keepdims=True)
    second = jnp.mean(weighted * unit, axis=-1, keepdims=True)
    return inverse * (weighted - first - unit * second)


def gelu_both(v):
    square = v * v
    half = 0.5 + 0.5 * jnp.tanh(v * (0.7978845608 + 0.7978845608 * 0.044715 * square))
    steep = v * (1.5957691216 + 1.5957691216 * 0.134145 * square)
    return v * half, half + half * (steep * (1.0 - half))


def t_dot(a, b):
    return lax.dot_general(a, b, (((0,), (0,)), ((), ())), preferred_element_type=F32)


def after(value, *others):
    return lax.optimization_barrier((value,) + others)[0]


def dot(a, b):
    return jnp.dot(a, b, preferred_element_type=F32)

def dot_t(a, b):
    return lax.dot_general(a, b, (((1,), (1,)), ((), ())), preferred_element_type=F32)

def head_lanes(head, rows):
    lanes = lax.broadcasted_iota(jnp.int32, (rows, 2 * HEAD_DIM), 1)
    return (lanes < HEAD_DIM) if head == 0 else (lanes >= HEAD_DIM)

def keep_causal(scores, tile):
    keys = scores.shape[0]
    key_pos = lax.broadcasted_iota(jnp.int32, (tile, tile), 0)
    query_pos = lax.broadcasted_iota(jnp.int32, (tile, tile), 1)
    last = jnp.where(key_pos <= query_pos, scores[keys - tile :], NEGATIVE)
    if keys == tile:
        return last
    return jnp.concatenate([scores[: keys - tile], last], axis=0)

def attend_forward_kernel(tile, qkv_ref, out_ref, log_ref):
    rows = qkv_ref.shape[1]
    values_t = jnp.transpose(qkv_ref[2])
    for block in range(rows // tile):
        keys = (block + 1) * tile
        here = pl.ds(block * tile, tile)
        query_block = qkv_ref[0, here, :]
        pieces, logs = [], []
        for head in range(2):
            q = jnp.where(head_lanes(head, tile), query_block, jnp.zeros_like(query_block))
            scores = dot_t(qkv_ref[1, :keys, :], q) * (HEAD_DIM ** (-0.5))
            scores = keep_causal(scores, tile)
            top = jnp.max(scores, axis=0, keepdims=True)
            powers = jnp.exp(scores - top)
            total = jnp.sum(powers, axis=0, keepdims=True)
            blended = dot(values_t[head * HEAD_DIM : (head + 1) * HEAD_DIM, :keys], powers.astype(BF))
            pieces.append(blended / total)
            logs.append(top + jnp.log(total))
        out_ref[here, :] = jnp.transpose(jnp.concatenate(pieces, axis=0)).astype(BF)
        for head in range(2):
            log_ref[0, head : head + 1, here] = logs[head]

def attend_backward_kernel(tile, qkv_ref, log_ref, grad_ref, out_ref, key_acc, value_acc):
    rows = qkv_ref.shape[1]
    scale = HEAD_DIM ** (-0.5)
    keys_t = jnp.transpose(qkv_ref[1])
    count = rows // tile
    for block in reversed(range(count)):
        keys = (block + 1) * tile
        here = pl.ds(block * tile, tile)
        query_block = qkv_ref[0, here, :]
        grad_block = grad_ref[here, :]
        pieces = []
        for head in range(2):
            lanes = head_lanes(head, tile)
            q = jnp.where(lanes, query_block, jnp.zeros_like(query_block))
            g = jnp.where(lanes, grad_block, jnp.zeros_like(grad_block))
            scores = dot_t(qkv_ref[1, :keys, :], q) * scale
            scores = keep_causal(scores, tile)
            weights = jnp.exp(scores - log_ref[0, head : head + 1, here])
            weight_grad = dot_t(qkv_ref[2, :keys, :], g)
            inner = jnp.sum(weights * weight_grad, axis=0, keepdims=True)
            score_grad = (weights * (weight_grad - inner)).astype(BF)
            key_step = dot(score_grad, q)
            value_step = dot(weights.astype(BF), g)
            if block == count - 1 and head == 0:
                key_acc[...] = key_step
                value_acc[...] = value_step
            else:
                key_acc[:keys, :] += key_step
                value_acc[:keys, :] += value_step
            pieces.append(dot(keys_t[head * HEAD_DIM : (head + 1) * HEAD_DIM, :keys], score_grad))
        out_ref[0, here, :] = (jnp.transpose(jnp.concatenate(pieces, axis=0)) * scale).astype(BF)
    out_ref[1] = (key_acc[...] * scale).astype(BF)
    out_ref[2] = value_acc[...].astype(BF)

def attend_forward(qkv, tile=256):
    _, rows, columns = qkv.shape
    pairs = columns // (2 * HEAD_DIM)
    return pl.pallas_call(
        functools.partial(attend_forward_kernel, tile),
        grid=(pairs,),
        out_shape=(
            jax.ShapeDtypeStruct((rows, columns), BF),
            jax.ShapeDtypeStruct((pairs, 8, rows), F32),
        ),
        in_specs=[pl.BlockSpec((3, rows, 2 * HEAD_DIM), lambda p: (0, 0, p))],
        out_specs=(
            pl.BlockSpec((rows, 2 * HEAD_DIM), lambda p: (0, p)),
            pl.BlockSpec((1, 8, rows), lambda p: (p, 0, 0)),
        ),
        cost_estimate=pl.CostEstimate(
            flops=8 * rows * rows * columns // 2, bytes_accessed=8 * rows * columns,
            transcendentals=rows * rows * columns // 128),
        name="attend_forward",
    )(qkv)

def attend_backward(qkv, logs, grads, tile=256):
    _, rows, columns = qkv.shape
    pairs = columns // (2 * HEAD_DIM)
    return pl.pallas_call(
        functools.partial(attend_backward_kernel, tile),
        grid=(pairs,),
        out_shape=jax.ShapeDtypeStruct((3, rows, columns), BF),
        in_specs=[
            pl.BlockSpec((3, rows, 2 * HEAD_DIM), lambda p: (0, 0, p)),
            pl.BlockSpec((1, 8, rows), lambda p: (p, 0, 0)),
            pl.BlockSpec((rows, 2 * HEAD_DIM), lambda p: (0, p)),
        ],
        out_specs=pl.BlockSpec((3, rows, 2 * HEAD_DIM), lambda p: (0, 0, p)),
        scratch_shapes=[pltpu.VMEM((rows, 2 * HEAD_DIM), F32)] * 2,
        cost_estimate=pl.CostEstimate(
            flops=20 * rows * rows * columns // 2, bytes_accessed=16 * rows * columns,
            transcendentals=rows * rows * columns // 128),
        name="attend_backward",
    )(qkv, logs, grads)


def project_kernel(heads_ref, weight_ref, token_ref, gain_ref, shift_ref, rest_ref, low_ref):
    total = token_ref[...].astype(F32)
    for z in range(heads_ref.shape[0]):
        total = total + dot(heads_ref[z], weight_ref[z])
    rest_ref[...] = total
    unit, _ = norm_stats(total)
    low_ref[...] = (unit * gain_ref[...] + shift_ref[...]).astype(BF)


def project_norm(heads, weight, tokens, gain, shift, tile=256):
    parts, rows, columns = heads.shape
    width = weight.shape[2]
    block = lambda i: (i, 0)
    return pl.pallas_call(
        project_kernel,
        grid=(rows // tile,),
        out_shape=(
            jax.ShapeDtypeStruct((rows, width), F32),
            jax.ShapeDtypeStruct((rows, width), BF),
        ),
        in_specs=[
            pl.BlockSpec((parts, tile, columns), lambda i: (0, i, 0)),
            pl.BlockSpec((parts, columns, width), lambda i: (0, 0, 0)),
            pl.BlockSpec((tile, width), block),
            pl.BlockSpec((1, width), lambda i: (0, 0)),
            pl.BlockSpec((1, width), lambda i: (0, 0)),
        ],
        out_specs=(pl.BlockSpec((tile, width), block), pl.BlockSpec((tile, width), block)),
        cost_estimate=pl.CostEstimate(
            flops=2 * rows * parts * columns * width,
            bytes_accessed=12 * rows * width,
            transcendentals=rows,
        ),
        name="project_norm",
    )(heads, weight, tokens, gain[None], shift[None])


def gelu_back_kernel(
    rows_ref, up_ref, hidden_grad_ref, hidden_ref, pre_grad_ref, in_ref
):
    shape = rows_ref.shape
    count = shape[0] * shape[2]
    rows = rows_ref[...].reshape(count, shape[3])
    units = up_ref.shape[2]
    step = min(256, units)
    dots = None
    for start in range(0, units, step):
        here = slice(start, start + step)
        hidden, slope = gelu_both(dot(rows, up_ref[0, :, here]))
        hidden = hidden.astype(BF)
        hidden_ref[0, :, here] = hidden
        hidden_grad = hidden_grad_ref[0, :, here].astype(F32)
        pre_grad_ref[0, :, here] = (hidden_grad * slope).astype(BF)
        product = hidden.astype(F32) * hidden_grad
        for lane in range(0, step, 128):
            part = product[:, lane : lane + 128]
            dots = part if dots is None else dots + part
    in_rows = dot_t(pre_grad_ref[0], up_ref[0]).astype(BF)
    capacity = shape[2]
    for block in range(shape[0]):
        here = slice(block * capacity, (block + 1) * capacity)
        in_ref[block, 0, :capacity, :] = in_rows[here]
        total = jnp.sum(jnp.transpose(dots[here]), axis=0, keepdims=True)
        total = jnp.broadcast_to(total, (EXTRA, capacity))
        low = total - total.astype(BF).astype(F32)
        line = lax.broadcasted_iota(jnp.int32, total.shape, 0)
        both = jnp.where(line == 0, total, jnp.where(line == 1, low, 0.0))
        in_ref[block, 0, capacity:, :] = jnp.zeros((EXTRA, shape[3]), BF)
        in_ref[block, 0, capacity:, :capacity] = both.astype(BF)


def expert_back(arrived, expert_up, hidden_grads, tile=512):
    blocks, held, capacity, width = arrived.shape
    rows = blocks * capacity
    units = expert_up.shape[2]
    slots = lambda e, i: (i, e, 0, 0)
    flat = pl.BlockSpec((1, tile, units), lambda e, i: (e, i, 0))
    return pl.pallas_call(
        gelu_back_kernel,
        grid=(held, rows // tile),
        out_shape=(
            jax.ShapeDtypeStruct((held, rows, units), BF),
            jax.ShapeDtypeStruct((held, rows, units), BF),
            jax.ShapeDtypeStruct((blocks, held, capacity + EXTRA, width), BF),
        ),
        in_specs=[
            pl.BlockSpec((tile // capacity, 1, capacity, width), slots),
            pl.BlockSpec((1, width, units), lambda e, i: (e, 0, 0)),
            flat,
        ],
        out_specs=(
            flat,
            flat,
            pl.BlockSpec((tile // capacity, 1, capacity + EXTRA, width), slots),
        ),
        cost_estimate=pl.CostEstimate(
            flops=4 * held * rows * units * width,
            bytes_accessed=14 * held * rows * width,
            transcendentals=held * rows * units,
        ),
        name="expert_back",
    )(arrived, expert_up, hidden_grads)


def slot_rows_kernel(flat_ref, weight_ref, out_ref):
    out_ref[...] = dot(flat_ref[0], weight_ref[0]).astype(BF).reshape(out_ref.shape)


def slot_rows(flat, weight, blocks, tile=512):
    held, rows, depth = flat.shape
    capacity = rows // blocks
    columns = weight.shape[2]
    return pl.pallas_call(
        slot_rows_kernel,
        grid=(held, rows // tile),
        out_shape=jax.ShapeDtypeStruct((blocks, held, capacity, columns), BF),
        in_specs=[
            pl.BlockSpec((1, tile, depth), lambda e, i: (e, i, 0)),
            pl.BlockSpec((1, depth, columns), lambda e, i: (e, 0, 0)),
        ],
        out_specs=pl.BlockSpec(
            (tile // capacity, 1, capacity, columns), lambda e, i: (i, e, 0, 0)
        ),
        cost_estimate=pl.CostEstimate(
            flops=2 * held * rows * depth * columns,
            bytes_accessed=4 * held * rows * (depth + columns),
            transcendentals=0,
        ),
        name="slot_rows",
    )(flat, weight)


def combine_kernel(place_ref, weight_ref, back_ref, base_ref, out_ref):
    tile, slots = place_ref.shape[0], back_ref.shape[0]
    pick = lax.broadcasted_iota(jnp.int32, (tile, slots), 1) == place_ref[...]
    rows = dot(pick.astype(BF), back_ref[...])
    out_ref[...] = (base_ref[...] + weight_ref[...] * rows).astype(BF)


def combine(place, weight, back, base, urgency=1, tile=256):
    slots, columns = back.shape
    rows = base.shape[0]
    own = pl.BlockSpec((tile, 1), lambda i: (i, 0))
    return pl.pallas_call(
        combine_kernel,
        grid=(rows // tile,),
        out_shape=jax.ShapeDtypeStruct((rows, columns), BF),
        in_specs=[
            own,
            own,
            pl.BlockSpec((slots, columns), lambda i: (0, 0)),
            pl.BlockSpec((tile, columns), lambda i: (i, 0)),
        ],
        out_specs=pl.BlockSpec((tile, columns), lambda i: (i, 0)),
        cost_estimate=pl.CostEstimate(
            flops=2 * rows * slots * columns * urgency,
            bytes_accessed=2 * slots * columns + 6 * rows * columns,
            transcendentals=0,
        ),
        name="combine",
    )(place, weight, back, base)


def hidden_grad_kernel(grads_ref, down_ref, out_ref):
    shape = grads_ref.shape
    rows = grads_ref[...].reshape(shape[0] * shape[2], shape[3])
    out_ref[0] = dot_t(rows, down_ref[0]).astype(BF)


def expert_hidden_grad(cotan_slots, expert_down, tile=512):
    blocks, held, capacity, width = cotan_slots.shape
    rows = blocks * capacity
    units = expert_down.shape[1]
    return pl.pallas_call(
        hidden_grad_kernel,
        grid=(held, rows // tile),
        out_shape=jax.ShapeDtypeStruct((held, rows, units), BF),
        in_specs=[
            pl.BlockSpec((tile // capacity, 1, capacity, width), lambda e, i: (i, e, 0, 0)),
            pl.BlockSpec((1, units, width), lambda e, i: (e, 0, 0)),
        ],
        out_specs=pl.BlockSpec((1, tile, units), lambda e, i: (e, i, 0)),
        cost_estimate=pl.CostEstimate(
            flops=2 * held * rows * units * width,
            bytes_accessed=6 * held * rows * width,
            transcendentals=0,
        ),
        name="expert_hidden_grad",
    )(cotan_slots, expert_down)


def normed_kernel(grad_ref, weight_ref, token_ref, out_ref, sums_ref):
    total = dot_t(grad_ref[0], weight_ref[0])
    for c in range(1, grad_ref.shape[0]):
        total = total + dot_t(grad_ref[c], weight_ref[c])
    out_ref[...] = total.astype(BF)
    unit, _ = norm_stats(token_ref[...].astype(F32))

    @pl.when(pl.program_id(0) == 0)
    def _():
        sums_ref[...] = jnp.zeros_like(sums_ref)

    sums_ref[0:1, :] += jnp.sum(total * unit, axis=0, keepdims=True)
    sums_ref[1:2, :] += jnp.sum(total, axis=0, keepdims=True)


def normed_back(qkv_grad, project_in, tokens, tile=256):
    count, rows, columns = qkv_grad.shape
    width = project_in.shape[1]
    return pl.pallas_call(
        normed_kernel,
        grid=(rows // tile,),
        out_shape=(
            jax.ShapeDtypeStruct((rows, width), BF),
            jax.ShapeDtypeStruct((8, width), F32),
        ),
        in_specs=[
            pl.BlockSpec((count, tile, columns), lambda i: (0, i, 0)),
            pl.BlockSpec((count, width, columns), lambda i: (0, 0, 0)),
            pl.BlockSpec((tile, width), lambda i: (i, 0)),
        ],
        out_specs=(
            pl.BlockSpec((tile, width), lambda i: (i, 0)),
            pl.BlockSpec((8, width), lambda i: (0, 0)),
        ),
        cost_estimate=pl.CostEstimate(
            flops=2 * count * rows * columns * width,
            bytes_accessed=6 * rows * width,
            transcendentals=rows,
        ),
        name="normed_back",
    )(qkv_grad, project_in, tokens)


def mid_back_kernel(
    place_ref, grad_ref, gates_ref, rest_ref, cotan_ref, gain_ref, weight_ref,
    heads_ref, rest_grad_ref, low_ref, sums_ref,
):
    grad = grad_ref[...].astype(F32) + gates_ref[...]
    unit, inverse = norm_stats(rest_ref[...])
    rest_grad = cotan_ref[...].astype(F32) + norm_back(unit, inverse, gain_ref[...], grad)
    rest_grad_ref[...] = rest_grad
    low = rest_grad.astype(BF)
    low_ref[...] = low
    for z in range(weight_ref.shape[0]):
        heads_ref[z] = dot_t(low, weight_ref[z]).astype(BF)
    sums_ref[0:1, :] = jnp.sum(grad * unit, axis=0, keepdims=True)
    sums_ref[1:2, :] = jnp.sum(grad, axis=0, keepdims=True)


def mid_back(place, mid_grad, gates, residual, cotangent, gain, weight):
    parts, columns, width = weight.shape
    rows = mid_grad.shape[0]
    here = lambda i, place: (place[0], 0)
    whole = lambda i, place: (0, 0)
    cube = lambda i, place: (0, 0, 0)
    return pl.pallas_call(
        mid_back_kernel,
        grid_spec=pltpu.PrefetchScalarGridSpec(
            num_scalar_prefetch=1,
            grid=(1,),
            in_specs=[
                pl.BlockSpec((rows, width), whole),
                pl.BlockSpec((rows, width), whole),
                pl.BlockSpec((rows, width), here),
                pl.BlockSpec((rows, width), here),
                pl.BlockSpec((1, width), whole),
                pl.BlockSpec((parts, columns, width), cube),
            ],
            out_specs=(
                pl.BlockSpec((parts, rows, columns), cube),
                pl.BlockSpec((rows, width), whole),
                pl.BlockSpec((rows, width), whole),
                pl.BlockSpec((8, width), whole),
            ),
        ),
        out_shape=(
            jax.ShapeDtypeStruct((parts, rows, columns), BF),
            jax.ShapeDtypeStruct((rows, width), F32),
            jax.ShapeDtypeStruct((rows, width), BF),
            jax.ShapeDtypeStruct((8, width), F32),
        ),
        cost_estimate=pl.CostEstimate(
            flops=2 * rows * parts * columns * width,
            bytes_accessed=16 * rows * width,
            transcendentals=rows,
        ),
        name="mid_back",
    )(place[None], mid_grad, gates, residual, cotangent, gain[None], weight)


def local(
    tokens,
    cotangent,
    routes,
    slot_index,
    first_gain,
    first_shift,
    project_in,
    project_out,
    second_gain,
    second_shift,
    router_weight,
    mixing_weight,
    dense_up,
    dense_down,
    expert_up,
    expert_down,
):
    row_count, width = tokens.shape
    expert_count = router_weight.shape[1]
    capacity = 2 * row_count // expert_count
    held = expert_up.shape[0]
    blocks = expert_count // held
    slot_total = expert_count * capacity
    head_columns = project_in.shape[2]
    parts = lax.axis_size("tensor")
    part_rows = row_count // parts
    my_start = lax.axis_index("tensor") * part_rows

    def mine(rows, axis=0):
        return lax.dynamic_slice_in_dim(rows, my_start, part_rows, axis)

    z = lax.axis_index("tensor")

    def shift_tensor(pick):
        return [
            lax.ppermute(pick(k), "tensor", [(i, (i + k) % parts) for i in range(parts)])
            if k
            else pick(0)
            for k in range(parts)
        ]

    def scatter_tensor(rows):
        return shift_tensor(
            lambda k: lax.dynamic_index_in_dim(rows, (z + k) % parts, 0, keepdims=False)
        )

    def in_order(pieces):
        twice = jnp.stack(pieces[::-1] * 2)
        return lax.dynamic_slice_in_dim(twice, parts - 1 - z, parts, 0)

    place = lax.axis_index("expert")
    odd = place % 2
    far = place // 2 % 2
    quarter = head_columns // 4
    own = lax.dynamic_slice_in_dim(project_out, (2 * far + odd) * quarter, quarter, 0)
    own = lax.all_to_all(
        jnp.broadcast_to(own[None], (parts,) + own.shape), "tensor", 0, 0, tiled=True
    )
    project_in = jnp.swapaxes(project_in, 0, 1)
    unit_in, _ = norm_stats(tokens.astype(F32))
    normed_low = (unit_in * first_gain + first_shift).astype(BF)
    qkv = jnp.einsum("td,cdn->ctn", normed_low, project_in, preferred_element_type=F32).astype(BF)
    attended, log_total = attend_forward(qkv)
    attended_all = lax.all_gather(attended, "tensor", axis=0, tiled=True).reshape(
        parts, row_count, head_columns
    )
    pairs = [(i, i ^ 1) for i in range(blocks)]

    def from_pair(rows):
        return lax.ppermute(rows, "expert", pairs)

    def both_sides(side, own, other):
        return jnp.stack([jnp.where(side == 0, own, other), jnp.where(side == 0, other, own)])

    slot_place = jnp.where(slot_index < capacity, routes * capacity + slot_index, slot_total)
    slot_place = after(slot_place, attended)
    hit = lax.iota(jnp.int32, slot_total)[:, None] == slot_place[None, :]
    pick = hit.astype(BF)

    def to_slots(rows):
        return dot(pick, rows).astype(BF).reshape(blocks, held * capacity, width)

    def exchange(buffer):
        return lax.all_to_all(buffer, "expert", 0, 0, tiled=True)

    own_far = lax.ppermute(own, "expert", [(i, i ^ 2) for i in range(blocks)])
    cotan_sent, own_far = lax.optimization_barrier((to_slots(cotangent), own_far))
    cotan_slots = exchange(cotan_sent).reshape(blocks, held, capacity, width)
    own_sides = both_sides(far, own, own_far)
    project_out_all = jnp.transpose(both_sides(odd, own_sides, from_pair(own_sides)), (2, 1, 0, 3, 4))
    project_out_all = project_out_all.reshape(parts, head_columns, width)

    residual, mid_low = project_norm(
        attended_all, project_out_all, tokens, second_gain, second_shift
    )
    mid_slots = to_slots(mid_low)
    arrived = exchange(mid_slots).reshape(blocks, held, capacity, width)
    mid_low = after(mid_low, mid_slots, cotan_slots)
    router_logits = dot(mid_low, router_weight)
    mixing_logits = dot(mid_low, mixing_weight)
    router_probs = jax.nn.softmax(router_logits, axis=-1)
    mixing = jax.nn.softmax(mixing_logits, axis=-1)
    chosen = (routes[:, None] == lax.iota(jnp.int32, expert_count)[None, :]).astype(F32)
    gate = jnp.sum(chosen * router_probs, axis=-1, keepdims=True)
    dense_weight = mixing[:, 0:1]
    expert_weight = mixing[:, 1:2] * gate
    cotan = cotangent.astype(F32)

    dense_hidden, dense_slope = gelu_both(dot(mid_low, dense_up))
    dense_hidden = dense_hidden.astype(BF)
    dense_part = dot(dense_hidden, dense_down)
    dense_out_grad = (cotan * dense_weight).astype(BF)
    dense_pre_grad = (dot_t(dense_out_grad, dense_down) * dense_slope).astype(BF)
    mid_dense_part = dot_t(dense_pre_grad, dense_up)
    dense_down_grad = t_dot(dense_hidden, dense_out_grad)
    dense_up_grad = t_dot(mid_low, dense_pre_grad)
    dense_dot = jnp.sum(cotan * dense_part, axis=-1, keepdims=True)

    hidden_grads = expert_hidden_grad(after(cotan_slots, mid_slots), expert_down)
    slot_weight = jnp.sum(jnp.where(hit, expert_weight[:, 0][None, :], 0.0), axis=1)
    slot_weight = slot_weight.reshape(blocks, held * capacity)
    arrived, mid_dense_part, dense_dot, dense_up_grad, dense_down_grad = lax.optimization_barrier(
        (arrived, mid_dense_part, dense_dot, dense_up_grad, dense_down_grad)
    )
    hiddens, pre_grads, in_slots = expert_back(arrived, expert_up, hidden_grads)
    in_home = exchange(in_slots.reshape(blocks, held * (capacity + EXTRA), width))
    out_slots = slot_rows(after(hiddens, in_slots), expert_down, blocks)
    in_home, out_slots = lax.optimization_barrier((in_home, out_slots))
    out_home = exchange(out_slots.reshape(blocks, held * capacity, width))

    out_base = dense_weight * dense_part
    place_column = slot_place[:, None]
    tail_column = jnp.where(
        slot_index < capacity, routes * (capacity + EXTRA) + slot_index,
        expert_count * (capacity + EXTRA),
    )[:, None]

    def sum_rows(rows):
        return lax.psum_scatter(rows, "tensor", scatter_dimension=0, tiled=True)

    mid_part = combine(
        tail_column,
        expert_weight,
        in_home.reshape(expert_count * (capacity + EXTRA), width),
        mid_dense_part,
    )
    mid_grad = sum_rows(mid_part)
    out_part = combine(
        place_column,
        expert_weight,
        after(out_home, mid_part).reshape(slot_total, width),
        out_base,
        urgency=8,
    )
    out_sum = sum_rows(after(out_part, mid_part))
    mid_grad = after(mid_grad, out_part)

    slot_dot = after(in_home, mid_part).reshape(
        blocks, held, capacity + EXTRA, width
    )[:, :, capacity : capacity + 2, :capacity]
    slot_dot = jnp.sum(slot_dot.astype(F32), axis=2).reshape(slot_total)
    expert_dot = jnp.sum(jnp.where(hit, slot_dot[:, None], 0.0), axis=0)
    dots = jnp.stack([dense_dot[:, 0], expert_dot]).reshape(2, parts, part_rows)
    dots = sum(scatter_tensor(jnp.swapaxes(dots, 0, 1)))[:, :, None]
    dense_dot, expert_dot = dots[0], dots[1]
    gate_mine, mixing_mine = mine(gate), mine(mixing)
    gated_dot = gate_mine * expert_dot
    mean_dot = mixing_mine[:, 0:1] * dense_dot + mixing_mine[:, 1:2] * gated_dot
    mixing_low = (
        mixing_mine * (jnp.concatenate([dense_dot, gated_dot], axis=1) - mean_dot)
    ).astype(BF)
    router_low = (
        mixing_mine[:, 1:2] * gated_dot * (mine(chosen) - mine(router_probs))
    ).astype(BF)
    gates_mine = dot_t(router_low, router_weight) + dot_t(mixing_low, mixing_weight)

    chips = blocks // 2
    same_core = [[2 * i + core for i in range(chips)] for core in range(2)]

    def exchange_chips(buffer):
        return lax.all_to_all(
            buffer, "expert", 0, 0, tiled=True, axis_index_groups=same_core
        )

    def split(rows):
        return rows.reshape(2, chips, -1, width)

    def pair_sum(rows):
        sent = lax.dynamic_index_in_dim(rows, 1 - odd, 0, keepdims=False)
        kept = lax.dynamic_index_in_dim(rows, odd, 0, keepdims=False)
        return (kept.astype(F32) + from_pair(sent).astype(F32)).astype(BF)

    def spread(piece):
        got = jnp.stack(
            [piece]
            + [
                lax.ppermute(piece, "expert", [(i, i ^ (2 * k)) for i in range(blocks)])
                for k in range(1, chips)
            ]
        )
        bit = 1
        while bit < chips:
            sides = got.reshape(chips // (2 * bit), 2, bit, *piece.shape)
            swap = place // 2 // bit % 2
            got = jnp.where(swap == 0, sides, sides[:, ::-1]).reshape(chips, *piece.shape)
            bit *= 2
        return got, from_pair(got)

    dense_half = pair_sum(
        jnp.concatenate([split(dense_up_grad.astype(BF)), split(dense_down_grad.astype(BF))], axis=2)
    )

    attended_grad, residual_grad, attn_grad_low, second_sums = mid_back(
        lax.axis_index("tensor"),
        mid_grad,
        gates_mine,
        residual,
        cotangent,
        second_gain,
        project_out_all,
    )
    attended_grad_sent = attended_grad
    pieces = scatter_tensor(attended_grad)
    dense_got = exchange_chips(after(dense_half, pieces[1]))
    attended_grad = in_order(pieces).reshape(row_count, head_columns)
    project_out_grad = jnp.einsum(
        "ztn,td->znd",
        mine(attended_all, 1),
        after(attn_grad_low, attended_grad_sent),
        preferred_element_type=F32,
    ).astype(BF)
    dense_piece = jnp.sum(after(dense_got, attended_grad_sent).astype(F32), axis=0).astype(BF)
    qkv_grad = attend_backward(qkv, log_total, attended_grad)
    late_residual, late_sum = lax.optimization_barrier(
        (residual, out_sum, qkv_grad)
    )[:2]
    layer_mine = (mine(late_residual) + late_sum.astype(F32)).astype(BF)
    normed_low_part, first_sums = normed_back(after(qkv_grad, dense_got, layer_mine), project_in, tokens)
    slot_weight = exchange(after(slot_weight, normed_low_part)).reshape(blocks, held, capacity)
    layer_out = lax.all_gather(layer_mine, "tensor", axis=0, tiled=True)
    normed_grad = lax.psum_scatter(
        after(normed_low_part, layer_mine), "tensor", scatter_dimension=0, tiled=True
    )
    project_in_grad = (
        jnp.einsum(
            "ctn,td->cnd", after(qkv_grad, normed_low_part), normed_low,
            preferred_element_type=F32,
        )
        .astype(BF)
        .reshape(3 * head_columns, width)
    )
    small = jnp.concatenate(
        [
            first_sums[:2],
            second_sums[:2],
            t_dot(after(router_low, attended_grad_sent), mine(mid_low)),
            t_dot(after(mixing_low, attended_grad_sent), mine(mid_low)),
        ],
        axis=0,
    )
    each = -(-small.shape[0] // blocks)
    small = jnp.pad(small, ((0, each * blocks - small.shape[0]), (0, 0)))
    small = jnp.pad(small.reshape(blocks, each, width), ((0, 0), (0, 16 - each), (0, 0)))
    out_rows = head_columns // blocks
    rest = jnp.concatenate(
        [
            split(project_in_grad),
            jnp.transpose(
                project_out_grad.reshape(parts, 2, chips, out_rows, width), (1, 2, 0, 3, 4)
            ).reshape(2, chips, parts * out_rows, width),
            split(small.astype(BF)),
        ],
        axis=2,
    )
    rest_half = pair_sum(rest)
    rest_got = exchange_chips(after(rest_half, dense_piece, slot_weight))
    rest_piece = jnp.sum(rest_got.astype(F32), axis=0).astype(BF)
    dense = exchange_chips(
        jnp.broadcast_to(after(dense_piece, rest_piece)[None], (chips,) + dense_piece.shape)
    )

    expert_rows = [
        (
            arrived[:, e].reshape(blocks * capacity, width),
            cotan_slots[:, e].reshape(blocks * capacity, width).astype(F32),
            slot_weight[:, e].reshape(blocks * capacity, 1),
        )
        for e in range(held)
    ]
    expert_down_grad = jnp.stack(
        [
            t_dot(hiddens[e], (grads * after(row_weight, rest_half)).astype(BF))
            for e, (_, grads, row_weight) in enumerate(expert_rows)
        ]
    )
    normed_grad, expert_down_grad = lax.optimization_barrier(
        (normed_grad, expert_down_grad, layer_out, dense)
    )[:2]
    normed_grad = normed_grad.astype(F32)
    unit_first, inverse_first = norm_stats(mine(tokens).astype(F32))
    input_mine = residual_grad + norm_back(unit_first, inverse_first, first_gain, normed_grad)
    input_mine = input_mine.astype(BF)
    input_grad = lax.all_gather(input_mine, "tensor", axis=0, tiled=True)
    expert_up_grad = jnp.stack(
        [
            t_dot(
                rows, (pre_grads[e].astype(F32) * after(row_weight, input_mine)).astype(BF)
            )
            for e, (rows, _, row_weight) in enumerate(expert_rows)
        ]
    )

    in_rows = 3 * out_rows
    across = jnp.concatenate(
        [
            rest_piece[in_rows:-16].reshape(parts, out_rows, width),
            jnp.broadcast_to(rest_piece[None, -16:], (parts, 16, width)),
        ],
        axis=1,
    )
    across = after(scatter_tensor(across), input_mine)
    across = sum(piece.astype(F32) for piece in across).astype(BF)
    dense = after(dense, input_mine)
    dense_other = from_pair(dense)
    rest, rest_other = spread(jnp.concatenate([rest_piece[:in_rows], across], axis=0))
    rest = both_sides(odd, rest, rest_other).reshape(blocks, -1, width)
    dense = both_sides(odd, dense, dense_other).reshape(blocks, 2, -1, width)
    dense_up_grad = dense[:, 0].astype(F32).reshape(width, width)
    dense_down_grad = dense[:, 1].astype(F32).reshape(width, width)
    project_in_grad = rest[:, :in_rows].astype(F32).reshape(3, head_columns, width)
    project_in_grad = jnp.transpose(project_in_grad, (2, 0, 1))
    project_out_grad = rest[:, in_rows:-16].astype(F32).reshape(head_columns, width)
    small = rest[:, -16:][:, :each].astype(F32).reshape(blocks * each, width)

    return (
        layer_out,
        input_grad,
        small[0],
        small[1],
        project_in_grad,
        project_out_grad,
        small[2],
        small[3],
        small[4 : 4 + expert_count].T,
        small[4 + expert_count : 6 + expert_count].T,
        dense_up_grad,
        dense_down_grad,
        expert_up_grad,
        expert_down_grad,
    )


def solution(mesh):
    placed = (
        P("expert", None),
        P("expert", None),
        P("expert"),
        P("expert"),
        P(),
        P(),
        P(None, None, "tensor"),
        P("tensor", None),
        P(),
        P(),
        P(),
        P(),
        P(None, "tensor"),
        P("tensor", None),
        P("expert", None, "tensor"),
        P("expert", "tensor", None),
    )
    return jax.shard_map(
        local,
        mesh=mesh,
        in_specs=placed,
        out_specs=(
            P("expert", None),
            P("expert", None),
            P(),
            P(),
            P(None, None, "tensor"),
            P("tensor", None),
            P(),
            P(),
            P(),
            P(),
            P(None, "tensor"),
            P("tensor", None),
            P("expert", None, "tensor"),
            P("expert", "tensor", None),
        ),
        check_vma=False,
    )
```

```python
import functools

import jax
import jax.numpy as jnp
from jax import lax
from jax.experimental import pallas as pl
from jax.experimental.pallas import tpu as pltpu
from jax.sharding import PartitionSpec as P

HEAD_DIM = 64
EPS = 1e-05
NEGATIVE = -1e30
EXTRA = 8
BF = jnp.bfloat16
F32 = jnp.float32


def norm_stats(rows):
    row_mean = jnp.mean(rows, axis=-1, keepdims=True)
    centred = rows - row_mean
    spread = jnp.mean(centred * centred, axis=-1, keepdims=True)
    inverse = lax.rsqrt(spread + EPS)
    return centred * inverse, inverse


def norm_back(unit, inverse, gain, grad):
    weighted = grad * gain
    first = jnp.mean(weighted, axis=-1, keepdims=True)
    second = jnp.mean(weighted * unit, axis=-1, keepdims=True)
    return inverse * (weighted - first - unit * second)


def gelu_both(v):
    square = v * v
    half = 0.5 + 0.5 * jnp.tanh(v * (0.7978845608 + 0.7978845608 * 0.044715 * square))
    steep = v * (1.5957691216 + 1.5957691216 * 0.134145 * square)
    return v * half, half + half * (steep * (1.0 - half))


def t_dot(a, b):
    return lax.dot_general(a, b, (((0,), (0,)), ((), ())), preferred_element_type=F32)


def after(value, *others):
    return lax.optimization_barrier((value,) + others)[0]


def dot(a, b):
    return jnp.dot(a, b, preferred_element_type=F32)

def dot_t(a, b):
    return lax.dot_general(a, b, (((1,), (1,)), ((), ())), preferred_element_type=F32)

def head_lanes(head, rows):
    lanes = lax.broadcasted_iota(jnp.int32, (rows, 2 * HEAD_DIM), 1)
    return (lanes < HEAD_DIM) if head == 0 else (lanes >= HEAD_DIM)

def keep_causal(scores, tile):
    keys = scores.shape[0]
    key_pos = lax.broadcasted_iota(jnp.int32, (tile, tile), 0)
    query_pos = lax.broadcasted_iota(jnp.int32, (tile, tile), 1)
    last = jnp.where(key_pos <= query_pos, scores[keys - tile :], NEGATIVE)
    if keys == tile:
        return last
    return jnp.concatenate([scores[: keys - tile], last], axis=0)

def attend_forward_kernel(tile, qkv_ref, out_ref, log_ref):
    rows = qkv_ref.shape[1]
    values_t = jnp.transpose(qkv_ref[2])
    for block in range(rows // tile):
        keys = (block + 1) * tile
        here = pl.ds(block * tile, tile)
        query_block = qkv_ref[0, here, :]
        pieces, logs = [], []
        for head in range(2):
            q = jnp.where(head_lanes(head, tile), query_block, jnp.zeros_like(query_block))
            scores = dot_t(qkv_ref[1, :keys, :], q) * (HEAD_DIM ** (-0.5))
            scores = keep_causal(scores, tile)
            top = jnp.max(scores, axis=0, keepdims=True)
            powers = jnp.exp(scores - top)
            total = jnp.sum(powers, axis=0, keepdims=True)
            blended = dot(values_t[head * HEAD_DIM : (head + 1) * HEAD_DIM, :keys], powers.astype(BF))
            pieces.append(blended / total)
            logs.append(top + jnp.log(total))
        out_ref[here, :] = jnp.transpose(jnp.concatenate(pieces, axis=0)).astype(BF)
        for head in range(2):
            log_ref[0, head : head + 1, here] = logs[head]

def attend_backward_kernel(tile, qkv_ref, log_ref, grad_ref, out_ref, key_acc, value_acc):
    rows = qkv_ref.shape[1]
    scale = HEAD_DIM ** (-0.5)
    keys_t = jnp.transpose(qkv_ref[1])
    count = rows // tile
    for block in reversed(range(count)):
        keys = (block + 1) * tile
        here = pl.ds(block * tile, tile)
        query_block = qkv_ref[0, here, :]
        grad_block = grad_ref[here, :]
        pieces = []
        for head in range(2):
            lanes = head_lanes(head, tile)
            q = jnp.where(lanes, query_block, jnp.zeros_like(query_block))
            g = jnp.where(lanes, grad_block, jnp.zeros_like(grad_block))
            scores = dot_t(qkv_ref[1, :keys, :], q) * scale
            scores = keep_causal(scores, tile)
            weights = jnp.exp(scores - log_ref[0, head : head + 1, here])
            weight_grad = dot_t(qkv_ref[2, :keys, :], g)
            inner = jnp.sum(weights * weight_grad, axis=0, keepdims=True)
            score_grad = (weights * (weight_grad - inner)).astype(BF)
            key_step = dot(score_grad, q)
            value_step = dot(weights.astype(BF), g)
            if block == count - 1 and head == 0:
                key_acc[...] = key_step
                value_acc[...] = value_step
            else:
                key_acc[:keys, :] += key_step
                value_acc[:keys, :] += value_step
            pieces.append(dot(keys_t[head * HEAD_DIM : (head + 1) * HEAD_DIM, :keys], score_grad))
        out_ref[0, here, :] = (jnp.transpose(jnp.concatenate(pieces, axis=0)) * scale).astype(BF)
    out_ref[1] = (key_acc[...] * scale).astype(BF)
    out_ref[2] = value_acc[...].astype(BF)

def attend_forward(qkv, tile=256):
    _, rows, columns = qkv.shape
    pairs = columns // (2 * HEAD_DIM)
    return pl.pallas_call(
        functools.partial(attend_forward_kernel, tile),
        grid=(pairs,),
        out_shape=(
            jax.ShapeDtypeStruct((rows, columns), BF),
            jax.ShapeDtypeStruct((pairs, 8, rows), F32),
        ),
        in_specs=[pl.BlockSpec((3, rows, 2 * HEAD_DIM), lambda p: (0, 0, p))],
        out_specs=(
            pl.BlockSpec((rows, 2 * HEAD_DIM), lambda p: (0, p)),
            pl.BlockSpec((1, 8, rows), lambda p: (p, 0, 0)),
        ),
        cost_estimate=pl.CostEstimate(
            flops=8 * rows * rows * columns // 2, bytes_accessed=8 * rows * columns,
            transcendentals=rows * rows * columns // 128),
        name="attend_forward",
    )(qkv)

def attend_backward(qkv, logs, grads, tile=256):
    _, rows, columns = qkv.shape
    pairs = columns // (2 * HEAD_DIM)
    return pl.pallas_call(
        functools.partial(attend_backward_kernel, tile),
        grid=(pairs,),
        out_shape=jax.ShapeDtypeStruct((3, rows, columns), BF),
        in_specs=[
            pl.BlockSpec((3, rows, 2 * HEAD_DIM), lambda p: (0, 0, p)),
            pl.BlockSpec((1, 8, rows), lambda p: (p, 0, 0)),
            pl.BlockSpec((rows, 2 * HEAD_DIM), lambda p: (0, p)),
        ],
        out_specs=pl.BlockSpec((3, rows, 2 * HEAD_DIM), lambda p: (0, 0, p)),
        scratch_shapes=[pltpu.VMEM((rows, 2 * HEAD_DIM), F32)] * 2,
        cost_estimate=pl.CostEstimate(
            flops=20 * rows * rows * columns // 2, bytes_accessed=16 * rows * columns,
            transcendentals=rows * rows * columns // 128),
        name="attend_backward",
    )(qkv, logs, grads)


def project_kernel(heads_ref, weight_ref, token_ref, gain_ref, shift_ref, rest_ref, low_ref):
    total = token_ref[...].astype(F32)
    for z in range(heads_ref.shape[0]):
        total = total + dot(heads_ref[z], weight_ref[z])
    rest_ref[...] = total
    unit, _ = norm_stats(total)
    low_ref[...] = (unit * gain_ref[...] + shift_ref[...]).astype(BF)


def project_norm(heads, weight, tokens, gain, shift, tile=256):
    parts, rows, columns = heads.shape
    width = weight.shape[2]
    block = lambda i: (i, 0)
    return pl.pallas_call(
        project_kernel,
        grid=(rows // tile,),
        out_shape=(
            jax.ShapeDtypeStruct((rows, width), F32),
            jax.ShapeDtypeStruct((rows, width), BF),
        ),
        in_specs=[
            pl.BlockSpec((parts, tile, columns), lambda i: (0, i, 0)),
            pl.BlockSpec((parts, columns, width), lambda i: (0, 0, 0)),
            pl.BlockSpec((tile, width), block),
            pl.BlockSpec((1, width), lambda i: (0, 0)),
            pl.BlockSpec((1, width), lambda i: (0, 0)),
        ],
        out_specs=(pl.BlockSpec((tile, width), block), pl.BlockSpec((tile, width), block)),
        cost_estimate=pl.CostEstimate(
            flops=2 * rows * parts * columns * width,
            bytes_accessed=12 * rows * width,
            transcendentals=rows,
        ),
        name="project_norm",
    )(heads, weight, tokens, gain[None], shift[None])


def gelu_back_kernel(
    rows_ref, up_ref, hidden_grad_ref, hidden_ref, pre_grad_ref, in_ref
):
    shape = rows_ref.shape
    count = shape[0] * shape[2]
    rows = rows_ref[...].reshape(count, shape[3])
    units = up_ref.shape[2]
    step = min(256, units)
    dots = None
    for start in range(0, units, step):
        here = slice(start, start + step)
        hidden, slope = gelu_both(dot(rows, up_ref[0, :, here]))
        hidden = hidden.astype(BF)
        hidden_ref[0, :, here] = hidden
        hidden_grad = hidden_grad_ref[0, :, here].astype(F32)
        pre_grad_ref[0, :, here] = (hidden_grad * slope).astype(BF)
        product = hidden.astype(F32) * hidden_grad
        for lane in range(0, step, 128):
            part = product[:, lane : lane + 128]
            dots = part if dots is None else dots + part
    in_rows = dot_t(pre_grad_ref[0], up_ref[0]).astype(BF)
    capacity = shape[2]
    for block in range(shape[0]):
        here = slice(block * capacity, (block + 1) * capacity)
        in_ref[block, 0, :capacity, :] = in_rows[here]
        total = jnp.sum(jnp.transpose(dots[here]), axis=0, keepdims=True)
        total = jnp.broadcast_to(total, (EXTRA, capacity))
        low = total - total.astype(BF).astype(F32)
        line = lax.broadcasted_iota(jnp.int32, total.shape, 0)
        both = jnp.where(line == 0, total, jnp.where(line == 1, low, 0.0))
        in_ref[block, 0, capacity:, :] = jnp.zeros((EXTRA, shape[3]), BF)
        in_ref[block, 0, capacity:, :capacity] = both.astype(BF)


def expert_back(arrived, expert_up, hidden_grads, tile=512):
    blocks, held, capacity, width = arrived.shape
    rows = blocks * capacity
    units = expert_up.shape[2]
    slots = lambda e, i: (i, e, 0, 0)
    flat = pl.BlockSpec((1, tile, units), lambda e, i: (e, i, 0))
    return pl.pallas_call(
        gelu_back_kernel,
        grid=(held, rows // tile),
        out_shape=(
            jax.ShapeDtypeStruct((held, rows, units), BF),
            jax.ShapeDtypeStruct((held, rows, units), BF),
            jax.ShapeDtypeStruct((blocks, held, capacity + EXTRA, width), BF),
        ),
        in_specs=[
            pl.BlockSpec((tile // capacity, 1, capacity, width), slots),
            pl.BlockSpec((1, width, units), lambda e, i: (e, 0, 0)),
            flat,
        ],
        out_specs=(
            flat,
            flat,
            pl.BlockSpec((tile // capacity, 1, capacity + EXTRA, width), slots),
        ),
        cost_estimate=pl.CostEstimate(
            flops=4 * held * rows * units * width,
            bytes_accessed=14 * held * rows * width,
            transcendentals=held * rows * units,
        ),
        name="expert_back",
    )(arrived, expert_up, hidden_grads)


def slot_rows_kernel(flat_ref, weight_ref, out_ref):
    out_ref[...] = dot(flat_ref[0], weight_ref[0]).astype(BF).reshape(out_ref.shape)


def slot_rows(flat, weight, blocks, tile=512):
    held, rows, depth = flat.shape
    capacity = rows // blocks
    columns = weight.shape[2]
    return pl.pallas_call(
        slot_rows_kernel,
        grid=(held, rows // tile),
        out_shape=jax.ShapeDtypeStruct((blocks, held, capacity, columns), BF),
        in_specs=[
            pl.BlockSpec((1, tile, depth), lambda e, i: (e, i, 0)),
            pl.BlockSpec((1, depth, columns), lambda e, i: (e, 0, 0)),
        ],
        out_specs=pl.BlockSpec(
            (tile // capacity, 1, capacity, columns), lambda e, i: (i, e, 0, 0)
        ),
        cost_estimate=pl.CostEstimate(
            flops=2 * held * rows * depth * columns,
            bytes_accessed=4 * held * rows * (depth + columns),
            transcendentals=0,
        ),
        name="slot_rows",
    )(flat, weight)


def combine_kernel(place_ref, weight_ref, back_ref, base_ref, out_ref):
    tile, slots = place_ref.shape[0], back_ref.shape[0]
    pick = lax.broadcasted_iota(jnp.int32, (tile, slots), 1) == place_ref[...]
    rows = dot(pick.astype(BF), back_ref[...])
    out_ref[...] = (base_ref[...] + weight_ref[...] * rows).astype(BF)


def combine(place, weight, back, base, urgency=1, tile=256):
    slots, columns = back.shape
    rows = base.shape[0]
    own = pl.BlockSpec((tile, 1), lambda i: (i, 0))
    return pl.pallas_call(
        combine_kernel,
        grid=(rows // tile,),
        out_shape=jax.ShapeDtypeStruct((rows, columns), BF),
        in_specs=[
            own,
            own,
            pl.BlockSpec((slots, columns), lambda i: (0, 0)),
            pl.BlockSpec((tile, columns), lambda i: (i, 0)),
        ],
        out_specs=pl.BlockSpec((tile, columns), lambda i: (i, 0)),
        cost_estimate=pl.CostEstimate(
            flops=2 * rows * slots * columns * urgency,
            bytes_accessed=2 * slots * columns + 6 * rows * columns,
            transcendentals=0,
        ),
        name="combine",
    )(place, weight, back, base)


def hidden_grad_kernel(grads_ref, down_ref, out_ref):
    shape = grads_ref.shape
    rows = grads_ref[...].reshape(shape[0] * shape[2], shape[3])
    out_ref[0] = dot_t(rows, down_ref[0]).astype(BF)


def expert_hidden_grad(cotan_slots, expert_down, tile=512):
    blocks, held, capacity, width = cotan_slots.shape
    rows = blocks * capacity
    units = expert_down.shape[1]
    return pl.pallas_call(
        hidden_grad_kernel,
        grid=(held, rows // tile),
        out_shape=jax.ShapeDtypeStruct((held, rows, units), BF),
        in_specs=[
            pl.BlockSpec((tile // capacity, 1, capacity, width), lambda e, i: (i, e, 0, 0)),
            pl.BlockSpec((1, units, width), lambda e, i: (e, 0, 0)),
        ],
        out_specs=pl.BlockSpec((1, tile, units), lambda e, i: (e, i, 0)),
        cost_estimate=pl.CostEstimate(
            flops=2 * held * rows * units * width,
            bytes_accessed=6 * held * rows * width,
            transcendentals=0,
        ),
        name="expert_hidden_grad",
    )(cotan_slots, expert_down)


def normed_kernel(grad_ref, weight_ref, token_ref, out_ref, sums_ref):
    total = dot_t(grad_ref[0], weight_ref[0])
    for c in range(1, grad_ref.shape[0]):
        total = total + dot_t(grad_ref[c], weight_ref[c])
    out_ref[...] = total.astype(BF)
    unit, _ = norm_stats(token_ref[...].astype(F32))

    @pl.when(pl.program_id(0) == 0)
    def _():
        sums_ref[...] = jnp.zeros_like(sums_ref)

    sums_ref[0:1, :] += jnp.sum(total * unit, axis=0, keepdims=True)
    sums_ref[1:2, :] += jnp.sum(total, axis=0, keepdims=True)


def normed_back(qkv_grad, project_in, tokens, tile=256):
    count, rows, columns = qkv_grad.shape
    width = project_in.shape[1]
    return pl.pallas_call(
        normed_kernel,
        grid=(rows // tile,),
        out_shape=(
            jax.ShapeDtypeStruct((rows, width), BF),
            jax.ShapeDtypeStruct((8, width), F32),
        ),
        in_specs=[
            pl.BlockSpec((count, tile, columns), lambda i: (0, i, 0)),
            pl.BlockSpec((count, width, columns), lambda i: (0, 0, 0)),
            pl.BlockSpec((tile, width), lambda i: (i, 0)),
        ],
        out_specs=(
            pl.BlockSpec((tile, width), lambda i: (i, 0)),
            pl.BlockSpec((8, width), lambda i: (0, 0)),
        ),
        cost_estimate=pl.CostEstimate(
            flops=2 * count * rows * columns * width,
            bytes_accessed=6 * rows * width,
            transcendentals=rows,
        ),
        name="normed_back",
    )(qkv_grad, project_in, tokens)


def mid_back_kernel(
    place_ref, grad_ref, gates_ref, rest_ref, cotan_ref, gain_ref, weight_ref,
    heads_ref, rest_grad_ref, low_ref, sums_ref,
):
    grad = grad_ref[...].astype(F32) + gates_ref[...]
    unit, inverse = norm_stats(rest_ref[...])
    rest_grad = cotan_ref[...].astype(F32) + norm_back(unit, inverse, gain_ref[...], grad)
    rest_grad_ref[...] = rest_grad
    low = rest_grad.astype(BF)
    low_ref[...] = low
    for z in range(weight_ref.shape[0]):
        heads_ref[z] = dot_t(low, weight_ref[z]).astype(BF)
    sums_ref[0:1, :] = jnp.sum(grad * unit, axis=0, keepdims=True)
    sums_ref[1:2, :] = jnp.sum(grad, axis=0, keepdims=True)


def mid_back(place, mid_grad, gates, residual, cotangent, gain, weight):
    parts, columns, width = weight.shape
    rows = mid_grad.shape[0]
    here = lambda i, place: (place[0], 0)
    whole = lambda i, place: (0, 0)
    cube = lambda i, place: (0, 0, 0)
    return pl.pallas_call(
        mid_back_kernel,
        grid_spec=pltpu.PrefetchScalarGridSpec(
            num_scalar_prefetch=1,
            grid=(1,),
            in_specs=[
                pl.BlockSpec((rows, width), whole),
                pl.BlockSpec((rows, width), whole),
                pl.BlockSpec((rows, width), here),
                pl.BlockSpec((rows, width), here),
                pl.BlockSpec((1, width), whole),
                pl.BlockSpec((parts, columns, width), cube),
            ],
            out_specs=(
                pl.BlockSpec((parts, rows, columns), cube),
                pl.BlockSpec((rows, width), whole),
                pl.BlockSpec((rows, width), whole),
                pl.BlockSpec((8, width), whole),
            ),
        ),
        out_shape=(
            jax.ShapeDtypeStruct((parts, rows, columns), BF),
            jax.ShapeDtypeStruct((rows, width), F32),
            jax.ShapeDtypeStruct((rows, width), BF),
            jax.ShapeDtypeStruct((8, width), F32),
        ),
        cost_estimate=pl.CostEstimate(
            flops=2 * rows * parts * columns * width,
            bytes_accessed=16 * rows * width,
            transcendentals=rows,
        ),
        name="mid_back",
    )(place[None], mid_grad, gates, residual, cotangent, gain[None], weight)


def local(
    tokens,
    cotangent,
    routes,
    slot_index,
    first_gain,
    first_shift,
    project_in,
    project_out,
    second_gain,
    second_shift,
    router_weight,
    mixing_weight,
    dense_up,
    dense_down,
    expert_up,
    expert_down,
):
    row_count, width = tokens.shape
    expert_count = router_weight.shape[1]
    capacity = 2 * row_count // expert_count
    held = expert_up.shape[0]
    blocks = expert_count // held
    slot_total = expert_count * capacity
    head_columns = project_in.shape[2]
    parts = lax.axis_size("tensor")
    part_rows = row_count // parts
    my_start = lax.axis_index("tensor") * part_rows

    def mine(rows, axis=0):
        return lax.dynamic_slice_in_dim(rows, my_start, part_rows, axis)

    z = lax.axis_index("tensor")

    def shift_tensor(pick):
        return [
            lax.ppermute(pick(k), "tensor", [(i, (i + k) % parts) for i in range(parts)])
            if k
            else pick(0)
            for k in range(parts)
        ]

    def scatter_tensor(rows):
        return shift_tensor(
            lambda k: lax.dynamic_index_in_dim(rows, (z + k) % parts, 0, keepdims=False)
        )

    def in_order(pieces):
        twice = jnp.stack(pieces[::-1] * 2)
        return lax.dynamic_slice_in_dim(twice, parts - 1 - z, parts, 0)

    place = lax.axis_index("expert")
    odd = place % 2
    far = place // 2 % 2
    quarter = head_columns // 4
    own = lax.dynamic_slice_in_dim(project_out, (2 * far + odd) * quarter, quarter, 0)
    own = lax.all_to_all(
        jnp.broadcast_to(own[None], (parts,) + own.shape), "tensor", 0, 0, tiled=True
    )
    project_in = jnp.swapaxes(project_in, 0, 1)
    unit_in, _ = norm_stats(tokens.astype(F32))
    normed_low = (unit_in * first_gain + first_shift).astype(BF)
    qkv = jnp.einsum("td,cdn->ctn", normed_low, project_in, preferred_element_type=F32).astype(BF)
    attended, log_total = attend_forward(qkv)
    attended_all = lax.all_gather(attended, "tensor", axis=0, tiled=True).reshape(
        parts, row_count, head_columns
    )
    pairs = [(i, i ^ 1) for i in range(blocks)]

    def from_pair(rows):
        return lax.ppermute(rows, "expert", pairs)

    def both_sides(side, own, other):
        return jnp.stack([jnp.where(side == 0, own, other), jnp.where(side == 0, other, own)])

    slot_place = jnp.where(slot_index < capacity, routes * capacity + slot_index, slot_total)
    slot_place = after(slot_place, attended)
    hit = lax.iota(jnp.int32, slot_total)[:, None] == slot_place[None, :]
    pick = hit.astype(BF)

    def to_slots(rows):
        return dot(pick, rows).astype(BF).reshape(blocks, held * capacity, width)

    def exchange(buffer):
        return lax.all_to_all(buffer, "expert", 0, 0, tiled=True)

    own_far = lax.ppermute(own, "expert", [(i, i ^ 2) for i in range(blocks)])
    cotan_sent, own_far = lax.optimization_barrier((to_slots(cotangent), own_far))
    cotan_slots = exchange(cotan_sent).reshape(blocks, held, capacity, width)
    own_sides = both_sides(far, own, own_far)
    project_out_all = jnp.transpose(both_sides(odd, own_sides, from_pair(own_sides)), (2, 1, 0, 3, 4))
    project_out_all = project_out_all.reshape(parts, head_columns, width)

    residual, mid_low = project_norm(
        attended_all, project_out_all, tokens, second_gain, second_shift
    )
    mid_slots = to_slots(mid_low)
    arrived = exchange(mid_slots).reshape(blocks, held, capacity, width)
    mid_low = after(mid_low, mid_slots, cotan_slots)
    router_logits = dot(mid_low, router_weight)
    mixing_logits = dot(mid_low, mixing_weight)
    router_probs = jax.nn.softmax(router_logits, axis=-1)
    mixing = jax.nn.softmax(mixing_logits, axis=-1)
    chosen = (routes[:, None] == lax.iota(jnp.int32, expert_count)[None, :]).astype(F32)
    gate = jnp.sum(chosen * router_probs, axis=-1, keepdims=True)
    dense_weight = mixing[:, 0:1]
    expert_weight = mixing[:, 1:2] * gate
    cotan = cotangent.astype(F32)

    dense_hidden, dense_slope = gelu_both(dot(mid_low, dense_up))
    dense_hidden = dense_hidden.astype(BF)
    dense_part = dot(dense_hidden, dense_down)
    dense_out_grad = (cotan * dense_weight).astype(BF)
    dense_pre_grad = (dot_t(dense_out_grad, dense_down) * dense_slope).astype(BF)
    mid_dense_part = dot_t(dense_pre_grad, dense_up)
    dense_down_grad = t_dot(dense_hidden, dense_out_grad)
    dense_up_grad = t_dot(mid_low, dense_pre_grad)
    dense_dot = jnp.sum(cotan * dense_part, axis=-1, keepdims=True)

    hidden_grads = expert_hidden_grad(after(cotan_slots, mid_slots), expert_down)
    slot_weight = jnp.sum(jnp.where(hit, expert_weight[:, 0][None, :], 0.0), axis=1)
    slot_weight = slot_weight.reshape(blocks, held * capacity)
    arrived, mid_dense_part, dense_dot, dense_up_grad, dense_down_grad = lax.optimization_barrier(
        (arrived, mid_dense_part, dense_dot, dense_up_grad, dense_down_grad)
    )
    hiddens, pre_grads, in_slots = expert_back(arrived, expert_up, hidden_grads)
    in_home = exchange(in_slots.reshape(blocks, held * (capacity + EXTRA), width))
    out_slots = slot_rows(after(hiddens, in_slots), expert_down, blocks)
    in_home, out_slots = lax.optimization_barrier((in_home, out_slots))
    out_home = exchange(out_slots.reshape(blocks, held * capacity, width))

    out_base = dense_weight * dense_part
    place_column = slot_place[:, None]
    tail_column = jnp.where(
        slot_index < capacity, routes * (capacity + EXTRA) + slot_index,
        expert_count * (capacity + EXTRA),
    )[:, None]

    def sum_rows(rows):
        return lax.psum_scatter(rows, "tensor", scatter_dimension=0, tiled=True)

    mid_part = combine(
        tail_column,
        expert_weight,
        in_home.reshape(expert_count * (capacity + EXTRA), width),
        mid_dense_part,
    )
    mid_grad = sum_rows(mid_part)
    out_part = combine(
        place_column,
        expert_weight,
        after(out_home, mid_part).reshape(slot_total, width),
        out_base,
        urgency=8,
    )
    out_sum = sum_rows(after(out_part, mid_part))
    mid_grad = after(mid_grad, out_part)

    slot_dot = after(in_home, mid_part).reshape(
        blocks, held, capacity + EXTRA, width
    )[:, :, capacity : capacity + 2, :capacity]
    slot_dot = jnp.sum(slot_dot.astype(F32), axis=2).reshape(slot_total)
    expert_dot = jnp.sum(jnp.where(hit, slot_dot[:, None], 0.0), axis=0)
    dots = jnp.stack([dense_dot[:, 0], expert_dot]).reshape(2, parts, part_rows)
    dots = sum(scatter_tensor(jnp.swapaxes(dots, 0, 1)))[:, :, None]
    dense_dot, expert_dot = dots[0], dots[1]
    gate_mine, mixing_mine = mine(gate), mine(mixing)
    gated_dot = gate_mine * expert_dot
    mean_dot = mixing_mine[:, 0:1] * dense_dot + mixing_mine[:, 1:2] * gated_dot
    mixing_low = (
        mixing_mine * (jnp.concatenate([dense_dot, gated_dot], axis=1) - mean_dot)
    ).astype(BF)
    router_low = (
        mixing_mine[:, 1:2] * gated_dot * (mine(chosen) - mine(router_probs))
    ).astype(BF)
    gates_mine = dot_t(router_low, router_weight) + dot_t(mixing_low, mixing_weight)

    chips = blocks // 2
    same_core = [[2 * i + core for i in range(chips)] for core in range(2)]

    def exchange_chips(buffer):
        return lax.all_to_all(
            buffer, "expert", 0, 0, tiled=True, axis_index_groups=same_core
        )

    def split(rows):
        return rows.reshape(2, chips, -1, width)

    def pair_sum(rows):
        sent = lax.dynamic_index_in_dim(rows, 1 - odd, 0, keepdims=False)
        kept = lax.dynamic_index_in_dim(rows, odd, 0, keepdims=False)
        return (kept.astype(F32) + from_pair(sent).astype(F32)).astype(BF)

    def spread(piece):
        got = jnp.stack(
            [piece]
            + [
                lax.ppermute(piece, "expert", [(i, i ^ (2 * k)) for i in range(blocks)])
                for k in range(1, chips)
            ]
        )
        bit = 1
        while bit < chips:
            sides = got.reshape(chips // (2 * bit), 2, bit, *piece.shape)
            swap = place // 2 // bit % 2
            got = jnp.where(swap == 0, sides, sides[:, ::-1]).reshape(chips, *piece.shape)
            bit *= 2
        return got, from_pair(got)

    dense_half = pair_sum(
        jnp.concatenate([split(dense_up_grad.astype(BF)), split(dense_down_grad.astype(BF))], axis=2)
    )

    attended_grad, residual_grad, attn_grad_low, second_sums = mid_back(
        lax.axis_index("tensor"),
        mid_grad,
        gates_mine,
        residual,
        cotangent,
        second_gain,
        project_out_all,
    )
    attended_grad_sent = attended_grad
    pieces = scatter_tensor(attended_grad)
    dense_got = exchange_chips(after(dense_half, pieces[1]))
    attended_grad = in_order(pieces).reshape(row_count, head_columns)
    project_out_grad = jnp.einsum(
        "ztn,td->znd",
        mine(attended_all, 1),
        after(attn_grad_low, attended_grad_sent),
        preferred_element_type=F32,
    ).astype(BF)
    dense_piece = jnp.sum(after(dense_got, attended_grad_sent).astype(F32), axis=0).astype(BF)
    qkv_grad = attend_backward(qkv, log_total, attended_grad)
    late_residual, late_sum = lax.optimization_barrier(
        (residual, out_sum, qkv_grad)
    )[:2]
    layer_mine = (mine(late_residual) + late_sum.astype(F32)).astype(BF)
    normed_low_part, first_sums = normed_back(after(qkv_grad, dense_got, layer_mine), project_in, tokens)
    slot_weight = exchange(after(slot_weight, normed_low_part)).reshape(blocks, held, capacity)
    layer_out = lax.all_gather(layer_mine, "tensor", axis=0, tiled=True)
    normed_grad = lax.psum_scatter(
        after(normed_low_part, layer_mine), "tensor", scatter_dimension=0, tiled=True
    )
    project_in_grad = (
        jnp.einsum(
            "ctn,td->cnd", after(qkv_grad, normed_low_part), normed_low,
            preferred_element_type=F32,
        )
        .astype(BF)
        .reshape(3 * head_columns, width)
    )
    small = jnp.concatenate(
        [
            first_sums[:2],
            second_sums[:2],
            t_dot(after(router_low, attended_grad_sent), mine(mid_low)),
            t_dot(after(mixing_low, attended_grad_sent), mine(mid_low)),
        ],
        axis=0,
    )
    each = -(-small.shape[0] // blocks)
    small = jnp.pad(small, ((0, each * blocks - small.shape[0]), (0, 0)))
    small = jnp.pad(small.reshape(blocks, each, width), ((0, 0), (0, 16 - each), (0, 0)))
    out_rows = head_columns // blocks
    rest = jnp.concatenate(
        [
            split(project_in_grad),
            jnp.transpose(
                project_out_grad.reshape(parts, 2, chips, out_rows, width), (1, 2, 0, 3, 4)
            ).reshape(2, chips, parts * out_rows, width),
            split(small.astype(BF)),
        ],
        axis=2,
    )
    rest_half = pair_sum(rest)
    rest_got = exchange_chips(after(rest_half, dense_piece, slot_weight))
    rest_piece = jnp.sum(rest_got.astype(F32), axis=0).astype(BF)
    dense = exchange_chips(
        jnp.broadcast_to(after(dense_piece, rest_piece)[None], (chips,) + dense_piece.shape)
    )

    expert_rows = [
        (
            arrived[:, e].reshape(blocks * capacity, width),
            cotan_slots[:, e].reshape(blocks * capacity, width).astype(F32),
            slot_weight[:, e].reshape(blocks * capacity, 1),
        )
        for e in range(held)
    ]
    down_grads = [
        t_dot(hiddens[e], (grads * after(row_weight, rest_half)).astype(BF))
        for e, (_, grads, row_weight) in enumerate(expert_rows)
    ]
    normed_grad, down_grads = lax.optimization_barrier(
        (normed_grad, down_grads, layer_out, dense)
    )[:2]
    normed_grad = normed_grad.astype(F32)
    unit_first, inverse_first = norm_stats(mine(tokens).astype(F32))
    input_mine = residual_grad + norm_back(unit_first, inverse_first, first_gain, normed_grad)
    input_mine = input_mine.astype(BF)
    input_grad = lax.all_gather(input_mine, "tensor", axis=0, tiled=True)
    expert_down_grad = jnp.stack(after(down_grads, input_mine))
    expert_up_grad = jnp.stack(
        [
            t_dot(
                rows, (pre_grads[e].astype(F32) * after(row_weight, input_mine)).astype(BF)
            )
            for e, (rows, _, row_weight) in enumerate(expert_rows)
        ]
    )

    in_rows = 3 * out_rows
    across = jnp.concatenate(
        [
            rest_piece[in_rows:-16].reshape(parts, out_rows, width),
            jnp.broadcast_to(rest_piece[None, -16:], (parts, 16, width)),
        ],
        axis=1,
    )
    across = after(scatter_tensor(across), input_mine)
    across = sum(piece.astype(F32) for piece in across).astype(BF)
    dense = after(dense, input_mine)
    dense_other = from_pair(dense)
    rest, rest_other = spread(jnp.concatenate([rest_piece[:in_rows], across], axis=0))
    rest = both_sides(odd, rest, rest_other).reshape(blocks, -1, width)
    dense = both_sides(odd, dense, dense_other).reshape(blocks, 2, -1, width)
    dense_up_grad = dense[:, 0].astype(F32).reshape(width, width)
    dense_down_grad = dense[:, 1].astype(F32).reshape(width, width)
    project_in_grad = rest[:, :in_rows].astype(F32).reshape(3, head_columns, width)
    project_in_grad = jnp.transpose(project_in_grad, (2, 0, 1))
    project_out_grad = rest[:, in_rows:-16].astype(F32).reshape(head_columns, width)
    small = rest[:, -16:][:, :each].astype(F32).reshape(blocks * each, width)

    return (
        layer_out,
        input_grad,
        small[0],
        small[1],
        project_in_grad,
        project_out_grad,
        small[2],
        small[3],
        small[4 : 4 + expert_count].T,
        small[4 + expert_count : 6 + expert_count].T,
        dense_up_grad,
        dense_down_grad,
        expert_up_grad,
        expert_down_grad,
    )


def solution(mesh):
    placed = (
        P("expert", None),
        P("expert", None),
        P("expert"),
        P("expert"),
        P(),
        P(),
        P(None, None, "tensor"),
        P("tensor", None),
        P(),
        P(),
        P(),
        P(),
        P(None, "tensor"),
        P("tensor", None),
        P("expert", None, "tensor"),
        P("expert", "tensor", None),
    )
    return jax.shard_map(
        local,
        mesh=mesh,
        in_specs=placed,
        out_specs=(
            P("expert", None),
            P("expert", None),
            P(),
            P(),
            P(None, None, "tensor"),
            P("tensor", None),
            P(),
            P(),
            P(),
            P(),
            P(None, "tensor"),
            P("tensor", None),
            P("expert", None, "tensor"),
            P("expert", "tensor", None),
        ),
        check_vma=False,
    )
```
